256 devices in a mesh: dp: 8 (over z), vocab: 32 (over y, x, core).
Axes of the slice: x: 4, y: 4, z: 8, core: 2. Of those that a mesh axis runs over, the one named last changes fastest.
Arguments:
- teacher_logits: bfloat16 [3072, 151552], P('dp', 'vocab'), may hold values from -40 to 320, as said below
- student_logits: bfloat16 [3072, 126976], P('dp', 'vocab'), may hold values from -40 to 320, as said below
- tile_dest: int32 [1184, 2], replicated, may hold values from 0 to 991, as said below
- tile_weight: bfloat16 [1184, 2, 128, 128], P('vocab'), may hold values from 0.0009994507 to 1
- token_mask: int32 [3072], P('dp'), may hold values from 0 to 1, as said below
Outputs:
- token_loss: float32 [3072], P('dp')
- mean_loss: float32 [], replicated
The draws below stay inside these ranges and needn't reach their ends.
Inputs may be any that keep to these rules, and one draw needn't show every extreme that they name: `teacher_logits`: Real-valued logits. `student_logits`: Real-valued logits. `tile_dest`: row b names the student blocks of the 2 tiles of teacher block b. Student block s belongs to vocab index s // 31, teacher block b to vocab index b // 37. Of the tiles of the teacher blocks of one vocab index, at most 3 name student blocks of any one vocab index, and exactly 3 do for some vocab index. `token_mask`: at least one token has a 1.
All inputs are finite; a program needn't handle non-finite values.
Results may differ from the reference program's by a relative error of at most 0.0031.
Values may be sent and summed in bfloat16 or wider, within the bound.
No kernel may reach another device: no remote copies, remote signals or barrier semaphores. Data moves between devices by JAX's collectives and lax.ppermute only.
A program may use at most 128 MiB of HBM per device.

```python
import math
import jax
import jax.numpy as jnp
from jax import lax

BLOCK = 128
VT = 151552
VS = 126976
K = 2
TOKENS = 3072
TBLOCKS = 1184
SBLOCKS = 992
TB_DEV = 37
SB_DEV = 31
CAP = 3
N_VOCAB = 32


def logit_field(key, row_count, col_count):
    key_base = jax.random.fold_in(key, 0)
    base_vals = jnp.clip(3.0 * jax.random.normal(key_base, (row_count, col_count), jnp.float32), -12.0, 12.0)
    return base_vals


def draw_teacher_logits(key, part):
    return logit_field(jax.random.fold_in(key, 11), TOKENS, VT).astype(jnp.bfloat16)


def draw_student_logits(key, part):
    return logit_field(jax.random.fold_in(key, 17), TOKENS, VS).astype(jnp.bfloat16)


def draw_tile_dest(key, part):
    tile_count = TB_DEV * K
    slot_count = N_VOCAB * CAP

    def one_source(source):
        sub_key = jax.random.fold_in(jax.random.fold_in(key, 29), source)
        key_score, key_pick, key_local = jax.random.split(sub_key, 3)
        position = jnp.arange(slot_count, dtype=jnp.int32)
        scores = jax.random.randint(key_score, (slot_count,), 0, 2 ** 20) * slot_count + position
        chosen = jax.random.randint(key_pick, (), 0, N_VOCAB)
        scores = jnp.where(position // CAP == chosen, scores - 2 ** 30, scores)
        slot_order = jnp.argsort(scores, stable=True)[:tile_count]
        owners = slot_order // CAP
        local_block = jax.random.randint(key_local, (tile_count,), 0, SB_DEV)
        return (owners * SB_DEV + local_block).astype(jnp.int32)
    sources = jax.vmap(one_source)(jnp.arange(N_VOCAB, dtype=jnp.int32))
    return sources.reshape(TBLOCKS, K)


def draw_token_mask(key, part):
    key_bits, key_keep = jax.random.split(jax.random.fold_in(key, 43))
    mask_vals = (jax.random.randint(key_bits, (TOKENS,), 0, 4) > 0).astype(jnp.int32)
    kept = jax.random.randint(key_keep, (), 0, TOKENS)
    position = jnp.arange(TOKENS, dtype=jnp.int32)
    return jnp.where(position == kept, 1, mask_vals).astype(jnp.int32)


def block_levels(stream_key, extent, pieces, smallest, largest):
    def one(dim, shards_of):
        heights = jax.random.uniform(jax.random.fold_in(jax.random.fold_in(stream_key, 6), dim), (shards_of,), jnp.float32, smallest / len(pieces), largest / len(pieces))
        return jnp.repeat(jnp.exp(heights), extent[dim] // shards_of).reshape((-1,) + (1,) * (len(extent) - dim - 1))

    loudness = one(*pieces[0])
    for cut in pieces[1:]:
        loudness = loudness * one(*cut)
    return loudness


def setup_inputs(seed: int = 0) -> dict:
    streams_of = jax.random.split(jax.random.key(seed), 6)
    return {
        "teacher_logits": draw_teacher_logits(jax.random.fold_in(streams_of[5], 71), 0),
        "student_logits": draw_student_logits(jax.random.fold_in(streams_of[5], 71), 0),
        "tile_dest": draw_tile_dest(jax.random.fold_in(streams_of[5], 71), 0),
        "tile_weight": jnp.clip(jnp.exp(math.log(1.0) - 6.9083047 * jax.random.uniform(streams_of[3], (TBLOCKS, K, BLOCK, BLOCK), jnp.float32) ** block_levels(streams_of[3], (TBLOCKS, K, BLOCK, BLOCK), ((0, 32),), -0.2, 0.2)), 0.0009994507, 1.0).astype(jnp.bfloat16),
        "token_mask": draw_token_mask(jax.random.fold_in(streams_of[5], 71), 0),
    }


SMOOTH = 0.1


def reference(teacher_logits, student_logits, tile_dest, tile_weight, token_mask):
    weights = tile_weight.astype(jnp.float32)
    mapping = (weights / jnp.sum(weights, axis=(1, 3), keepdims=True)).astype(jnp.bfloat16)
    mapping = lax.optimization_barrier(mapping).astype(jnp.float32)
    targets = tile_dest.reshape(-1).astype(jnp.int32)
    row_count = math.gcd(TOKENS, 256)

    def one_block(block_args):
        teacher_vals, student_vals, mask_vals = block_args
        teacher_vals = teacher_vals.astype(jnp.float32)
        maximum = jnp.max(teacher_vals, axis=1, keepdims=True)
        expon = jnp.exp(teacher_vals - maximum)
        teacher_prob = (expon / jnp.sum(expon, axis=1, keepdims=True)).astype(jnp.bfloat16)
        teacher_prob = lax.optimization_barrier(teacher_prob).astype(jnp.float32)
        prob_blocks = teacher_prob.reshape(row_count, TBLOCKS, BLOCK)
        partial_value = jnp.einsum('rbc,bkcd->bkrd', prob_blocks, mapping)
        partial_value = lax.optimization_barrier(partial_value.astype(jnp.bfloat16)).astype(jnp.float32)
        summed = jax.ops.segment_sum(partial_value.reshape(TBLOCKS * K, row_count, BLOCK), targets, num_segments=SBLOCKS)
        mapped = jnp.transpose(summed, (1, 0, 2)).reshape(row_count, VS)
        target = (1.0 - SMOOTH) * mapped + SMOOTH / VS
        student_vals = student_vals.astype(jnp.float32)
        student_max = jnp.max(student_vals, axis=1, keepdims=True)
        student_sum = jnp.sum(jnp.exp(student_vals - student_max), axis=1, keepdims=True)
        student_logp = student_vals - student_max - jnp.log(student_sum)
        token_kl = jnp.sum(target * (jnp.log(target) - student_logp), axis=1)
        return mask_vals.astype(jnp.float32) * token_kl

    token_loss = lax.map(one_block, (teacher_logits.reshape(-1, row_count, VT), student_logits.reshape(-1, row_count, VS), token_mask.reshape(-1, row_count)))
    token_loss = token_loss.reshape(TOKENS)
    counted = jnp.sum(token_mask.astype(jnp.float32))
    mean_loss = jnp.sum(token_loss) / counted
    return token_loss, mean_loss
```

```python
import functools

import jax
import jax.numpy as jnp
from jax import lax
from jax.experimental import pallas as pl
from jax.experimental.pallas import tpu as pltpu
from jax.sharding import PartitionSpec as P

BLOCK = 128
VS = 126976
K = 2
CAP = 3
SMOOTH = 0.1
LANES = 128
STAT_ROWS = 16
F32 = jnp.float32
BF16 = jnp.bfloat16


def iota(shape, dim):
    return lax.broadcasted_iota(jnp.int32, shape, dim)


def selector(mask_row, rows, first):
    tokens = mask_row.shape[1]
    before = (iota((tokens, tokens), 0) < iota((tokens, tokens), 1)).astype(F32).astype(BF16)
    kept = jnp.broadcast_to(mask_row.astype(F32), (16, tokens)).astype(BF16)
    rank = jnp.dot(kept, before, preferred_element_type=F32)[0:1]
    wanted = (iota((rows, tokens), 0) + first).astype(F32)
    hit = (wanted == jnp.broadcast_to(rank, (rows, tokens))) & (
        jnp.broadcast_to(mask_row, (rows, tokens)) > 0
    )
    return hit.astype(F32).astype(BF16)


def thirds(value):
    high = value.astype(BF16).astype(F32)
    middle = (value - high).astype(BF16).astype(F32)
    low = (value - high - middle).astype(BF16).astype(F32)
    return high, middle, low


def in_lanes(columns, rows):
    lane = iota((rows, LANES), 1)
    out = jnp.zeros((rows, LANES), F32)
    for v, column in enumerate(columns):
        if column is not None:
            out = jnp.where(lane == v, jnp.broadcast_to(column, (rows, LANES)), out)
    return out


def pieces_of(total, parts):
    cuts = [total * i // parts for i in range(parts + 1)]
    return list(zip(cuts[:-1], cuts[1:]))


def picked(sel_ref, src_ref, dst_ref, top_ref, blocks, waits):
    top_ref[...] = jnp.full(top_ref.shape, -jnp.inf, F32)

    def one(start, width):
        got = jnp.dot(sel_ref[...], src_ref[:, pl.ds(start, width)], preferred_element_type=F32)
        dst_ref[:, pl.ds(start, width)] = got.astype(BF16)
        top = top_ref[...]
        for i in range(width // BLOCK):
            top = jnp.maximum(top, got[:, i * BLOCK : (i + 1) * BLOCK])
        top_ref[...] = top

    for (lo, hi), wait in waits:
        wait()

        def body(i, carry):
            one(pl.multiple_of(i * 2 * BLOCK, 2 * BLOCK), 2 * BLOCK)
            return carry

        lax.fori_loop(lo, hi, body, 0)
    if blocks % 2:
        one((blocks - 1) * BLOCK, BLOCK)


def column_waits(hbm, buf, sems, blocks, parts):
    out = []
    runs = pieces_of(blocks // 2, parts)
    for c, (lo, hi) in enumerate(runs):
        end = hi * 2 * BLOCK if c < len(runs) - 1 else blocks * BLOCK
        where = (slice(None), pl.ds(lo * 2 * BLOCK, end - lo * 2 * BLOCK))
        copy = pltpu.make_async_copy(hbm.at[where], buf.at[where], sems.at[c])
        copy.start()
        out.append(((lo, hi), copy.wait))
    return out


def send_kernel(
    rows, first, sb_dev,
    me_ref, dest_ref, mask_ref, x_hbm, w_hbm, send_hbm,
    x_buf, w_buf, sel, xc, maps, stage, stat_cols, stat, top, total, used,
    w_sem, x_sem, out_sem, stat_sem,
):
    blocks = w_buf.shape[0]
    peers = send_hbm.shape[0]
    w_copy = pltpu.make_async_copy(w_hbm, w_buf, w_sem)
    w_copy.start()
    waits = column_waits(x_hbm, x_buf, x_sem, blocks, 4)
    sel[...] = selector(mask_ref[...], rows, first)

    def clear(i, carry):
        used[i] = 0
        return carry

    lax.fori_loop(0, peers, clear, 0)
    w_copy.wait()

    def weights(b, carry):
        both = jnp.concatenate([w_buf[b, k].astype(F32) for k in range(K)], axis=1)
        scale = 1.0 / jnp.sum(both, axis=1, keepdims=True)
        maps[b] = (both * scale).astype(BF16)
        return carry

    lax.fori_loop(0, blocks, weights, 0)
    picked(sel, x_buf, xc, top, blocks, waits)
    highest = jnp.max(top[...], axis=1, keepdims=True)
    top[...] = jnp.broadcast_to(highest, top.shape)
    total[...] = jnp.zeros(total.shape, F32)
    base = me_ref[0] * blocks

    def block(b, carry):
        raised = jnp.exp(xc[:, pl.ds(pl.multiple_of(b * BLOCK, BLOCK), BLOCK)].astype(F32) - top[...])
        total[...] += raised
        mapped = jnp.dot(raised.astype(BF16), maps[b], preferred_element_type=F32)
        for k in range(K):
            stage[K * b + k] = mapped[:, k * BLOCK : (k + 1) * BLOCK].astype(BF16)
            owner = lax.div(dest_ref[k, base + b], sb_dev)
            rank = used[owner]
            used[owner] = rank + 1
            pltpu.make_async_copy(
                stage.at[K * b + k],
                send_hbm.at[owner, pl.ds(pl.multiple_of(rank * rows, 16), rows)],
                out_sem.at[K * b + k],
            ).start()
        return carry

    lax.fori_loop(0, blocks, block, 0)
    summed = jnp.sum(total[...], axis=1, keepdims=True)
    stat_cols[...] = jnp.zeros(stat_cols.shape, F32)
    stat_cols[0:rows] = in_lanes((highest, *thirds(summed)), rows)
    for q in range(stat_cols.shape[0] // LANES):
        turned = stat_cols[q * LANES : (q + 1) * LANES].T
        stat[q * STAT_ROWS : (q + 1) * STAT_ROWS] = turned[:STAT_ROWS].astype(BF16)

    def stat_copy(d):
        return pltpu.make_async_copy(
            stat, send_hbm.at[d, pl.ds(CAP * rows, stat.shape[0])], stat_sem.at[d]
        )

    def stat_start(d, carry):
        stat_copy(d).start()
        return carry

    def stat_wait(d, carry):
        stat_copy(d).wait()
        return carry

    def tile_wait(i, carry):
        pltpu.make_async_copy(
            stage.at[i], send_hbm.at[0, pl.ds(0, rows)], out_sem.at[i]
        ).wait()
        return carry

    lax.fori_loop(0, peers, stat_start, 0)
    lax.fori_loop(0, K * blocks, tile_wait, 0)
    lax.fori_loop(0, peers, stat_wait, 0)


def student_kernel(
    rows, first, peers, tb_dev,
    me_ref, dest_ref, mask_ref, s_hbm,
    picked_ref, stat_ref, count_ref, slot_ref,
    s_buf, sel, cols, top, s_sem,
):
    blocks = s_buf.shape[1] // BLOCK
    waits = column_waits(s_hbm, s_buf, s_sem, blocks, 2)
    sel[...] = selector(mask_ref[...], rows, first)
    picked(sel, s_buf, picked_ref, top, blocks, waits)
    highest = jnp.max(top[...], axis=1, keepdims=True)

    def block(b, carry):
        at = pl.ds(pl.multiple_of(b * BLOCK, BLOCK), BLOCK)
        return carry + jnp.exp(picked_ref[:, at].astype(F32) - highest)

    total = lax.fori_loop(0, blocks, block, jnp.zeros((rows, BLOCK), F32))
    cols[...] = jnp.zeros(cols.shape, F32)
    cols[0:rows] = in_lanes((None, None, highest, jnp.sum(total, axis=1, keepdims=True)), rows)
    for q in range(cols.shape[0] // LANES):
        at = slice(q * LANES, (q + 1) * LANES)
        stat_ref[:, at] = cols[at].T[:8]

    def clear(i, carry):
        count_ref[i] = 0
        return carry

    lax.fori_loop(0, count_ref.shape[0], clear, 0)
    low = me_ref[0] * blocks

    def source(r, carry):
        def tile(b, rank):
            for k in range(K):
                near = dest_ref[k, r * tb_dev + b] - low
                mine = (near >= 0) & (near < blocks)

                @pl.when(mine)
                def _():
                    seen = count_ref[near]
                    slot_ref[near * (peers * CAP) + seen] = r * 4 + rank
                    count_ref[near] = seen + 1

                rank = rank + mine.astype(jnp.int32)
            return rank

        lax.fori_loop(0, tb_dev, tile, jnp.int32(0))
        return carry

    lax.fori_loop(0, peers, source, 0)


def combine_kernel(
    rows, chunk,
    count_ref, slot_ref, recv_hbm, s_ref, s_stat_ref, out_ref,
    buf, stat, stat32, share, spread, cols, sems, stat_sem,
):
    peers = recv_hbm.shape[0]
    blocks = s_ref.shape[1] // BLOCK
    stat_copy = pltpu.make_async_copy(
        recv_hbm.at[:, pl.ds(CAP * rows, stat.shape[1])], stat, stat_sem
    )
    stat_copy.start()
    copies = []
    for q in range(rows // chunk):
        for r in range(CAP):
            copy = pltpu.make_async_copy(
                recv_hbm.at[:, pl.ds(r * rows + q * chunk, chunk)],
                buf.at[r, :, pl.ds(q * chunk, chunk)],
                sems.at[q, r],
            )
            copy.start()
            copies.append(copy)
    stat_copy.wait()
    per = stat.shape[1]
    stat32[...] = stat[...].astype(F32).reshape(stat32.shape)
    for q in range(per // STAT_ROWS):
        highest, high, middle, low = (
            stat32[pl.ds(q * STAT_ROWS + v, peers, stride=per), :] for v in range(4)
        )
        raised = jnp.exp(highest - jnp.max(highest, axis=0, keepdims=True))
        total = jnp.sum(raised * ((high + middle) + low), axis=0, keepdims=True)
        part = raised * ((1.0 - SMOOTH) / total)
        padded = jnp.concatenate([part, jnp.zeros((LANES - peers, LANES), F32)], axis=0)
        share[q * LANES : (q + 1) * LANES] = padded.T
    cols[...] = jnp.zeros(cols.shape, F32)
    for q in range(rows // chunk):
        at = slice(q * chunk, (q + 1) * chunk)
        mine = share[at]
        for r in range(peers):
            spread[r] = jnp.broadcast_to(mine[:, r : r + 1], (chunk, LANES))
        for r in range(CAP):
            copies[q * CAP + r].wait()

        def block(j, carry):
            cross, mass = carry

            def add(n, acc):
                entry = slot_ref[j * (peers * CAP) + n]
                source = lax.shift_right_logical(entry, 2)
                piece = buf[entry & 3, source, at]
                return acc + spread[source] * piece.astype(F32)

            mapped = lax.fori_loop(0, count_ref[j], add, jnp.zeros((chunk, LANES), F32))
            target = mapped + SMOOTH / VS
            student = s_ref[at, pl.ds(pl.multiple_of(j * BLOCK, BLOCK), BLOCK)].astype(F32)
            return cross + target * (jnp.log(target) - student), mass + target

        zero = jnp.zeros((chunk, LANES), F32)
        cross, mass = lax.fori_loop(0, blocks, block, (zero, zero))
        cols[at] = in_lanes(
            (jnp.sum(cross, axis=1, keepdims=True), jnp.sum(mass, axis=1, keepdims=True)), chunk
        )
    for q in range(cols.shape[0] // LANES):
        at = slice(q * LANES, (q + 1) * LANES)
        values = cols[at].T[:8] + s_stat_ref[:, at]
        per = 8 * (cols.shape[0] // LANES)
        for d in range(peers):
            out_ref[d * per + q * 8 : d * per + (q + 1) * 8] = values


def loss_kernel(rows, first, all_ref, mask_ref, loss_ref, sums_ref):
    tokens = mask_ref.shape[1]
    spans = -(-tokens // LANES)
    peers = all_ref.shape[0] // (8 * spans)
    spread = []
    for q in range(spans):
        cross, mass, highest, sums = (
            all_ref[pl.ds(q * 8 + v, peers, stride=8 * spans), :] for v in range(4)
        )
        top = jnp.max(highest, axis=0, keepdims=True)
        total = jnp.sum(sums * jnp.exp(highest - top), axis=0, keepdims=True)
        norm = top + jnp.log(total)
        spread.append(
            jnp.sum(cross, axis=0, keepdims=True) + norm * jnp.sum(mass, axis=0, keepdims=True)
        )
    kl = jnp.concatenate(spread, axis=1)
    mask = mask_ref[...]
    counted = jnp.sum(mask.astype(F32), axis=1, keepdims=True)
    width = kl.shape[1]
    place = iota((1, width), 1)
    kl = jnp.where((place < rows) & ((place + first).astype(F32) < counted), kl, 0.0)
    row = iota((16, width), 0)
    parts = jnp.zeros((16, width), F32)
    for v, part in enumerate(thirds(kl)):
        parts = jnp.where(row == v, jnp.broadcast_to(part, (16, width)), parts)
    back = jnp.dot(parts.astype(BF16), selector(mask, width, first), preferred_element_type=F32)
    loss = jnp.sum(back, axis=0, keepdims=True) * mask.astype(F32)
    loss_ref[...] = loss
    lane = iota((8, LANES), 1)
    sums_ref[...] = jnp.where(
        lane == 0, jnp.sum(loss, axis=1, keepdims=True), jnp.where(lane == 1, counted, 0.0)
    )


def whole(memory_space):
    return pl.BlockSpec(memory_space=memory_space)


VM, SM, HB = pltpu.VMEM, pltpu.SMEM, pl.ANY


def exchanged(teacher_logits, student_logits, dest, tile_weight, mask, rows, first):
    peers = lax.axis_size("vocab")
    me = lax.axis_index("vocab").astype(jnp.int32).reshape(1)
    tokens = teacher_logits.shape[0]
    tb_dev = teacher_logits.shape[1] // BLOCK
    sb_dev = student_logits.shape[1] // BLOCK
    wide = -(-tokens // LANES) * LANES
    stat_rows = wide // LANES * STAT_ROWS
    tiles = tb_dev * K
    dma = pltpu.SemaphoreType.DMA
    send = pl.pallas_call(
        functools.partial(send_kernel, rows, first, sb_dev),
        out_shape=jax.ShapeDtypeStruct((peers, CAP * rows + stat_rows, LANES), BF16),
        in_specs=[whole(SM), whole(SM), whole(VM), whole(HB), whole(HB)],
        out_specs=whole(HB),
        scratch_shapes=[
            VM(teacher_logits.shape, BF16),
            VM(tile_weight.shape, BF16),
            VM((rows, tokens), BF16),
            VM((rows, tb_dev * BLOCK), BF16),
            VM((tb_dev, BLOCK, K * BLOCK), BF16),
            VM((tiles, rows, BLOCK), BF16),
            VM((wide, LANES), F32),
            VM((stat_rows, LANES), BF16),
            VM((rows, LANES), F32),
            VM((rows, LANES), F32),
            SM((peers,), jnp.int32),
            dma(()),
            dma((4,)),
            dma((tiles,)),
            dma((peers,)),
        ],
        compiler_params=pltpu.CompilerParams(vmem_limit_bytes=48 << 20),
        name="send",
    )(me, dest, mask, teacher_logits, tile_weight)
    received = lax.all_to_all(send, "vocab", 0, 0, tiled=True)
    kept, s_stat, counts, slots = pl.pallas_call(
        functools.partial(student_kernel, rows, first, peers, tb_dev),
        out_shape=(
            jax.ShapeDtypeStruct((rows, student_logits.shape[1]), BF16),
            jax.ShapeDtypeStruct((8, wide), F32),
            jax.ShapeDtypeStruct((sb_dev + 1,), jnp.int32),
            jax.ShapeDtypeStruct((sb_dev * peers * CAP,), jnp.int32),
        ),
        in_specs=[whole(SM), whole(SM), whole(VM), whole(HB)],
        out_specs=(whole(VM), whole(VM), whole(SM), whole(SM)),
        scratch_shapes=[
            VM(student_logits.shape, BF16),
            VM((rows, tokens), BF16),
            VM((wide, LANES), F32),
            VM((rows, LANES), F32),
            dma((2,)),
        ],
        compiler_params=pltpu.CompilerParams(vmem_limit_bytes=32 << 20),
        cost_estimate=pl.CostEstimate(
            flops=40 * 10**9, bytes_accessed=6 * 10**6, transcendentals=2 * 10**6
        ),
        name="student",
    )(me, dest, mask, student_logits)
    chunk = rows // 4 if rows % 64 == 0 else rows
    mine = pl.pallas_call(
        functools.partial(combine_kernel, rows, chunk),
        out_shape=jax.ShapeDtypeStruct((peers * 8 * (wide // LANES), LANES), F32),
        in_specs=[whole(SM), whole(SM), whole(HB), whole(VM), whole(VM)],
        out_specs=whole(VM),
        scratch_shapes=[
            VM((CAP, peers, rows, LANES), BF16),
            VM((peers, stat_rows, LANES), BF16),
            VM((peers * stat_rows, LANES), F32),
            VM((wide, LANES), F32),
            VM((peers, chunk, LANES), F32),
            VM((wide, LANES), F32),
            dma((rows // chunk, CAP)),
            dma(()),
        ],
        compiler_params=pltpu.CompilerParams(vmem_limit_bytes=40 << 20),
        name="combine",
    )(counts, slots, received, kept, s_stat)
    everyone = lax.all_to_all(mine, "vocab", 0, 0, tiled=True)
    return pl.pallas_call(
        functools.partial(loss_kernel, rows, first),
        out_shape=(
            jax.ShapeDtypeStruct((1, tokens), F32),
            jax.ShapeDtypeStruct((8, LANES), F32),
        ),
        in_specs=[whole(VM), whole(VM)],
        out_specs=(whole(VM), whole(VM)),
        name="loss",
    )(everyone, mask)


def summed_over(x, axis):
    size = lax.axis_size(axis)
    terms = [x] + [
        lax.ppermute(x, axis, [(i, i ^ flip) for i in range(size)]) for flip in range(1, size)
    ]
    while len(terms) > 1:
        terms = [a + b for a, b in zip(terms[::2], terms[1::2])]
    return terms[0]


def local(teacher_logits, student_logits, tile_dest, tile_weight, token_mask):
    tokens = teacher_logits.shape[0]
    loss, sums = exchanged(
        teacher_logits, student_logits, tile_dest.T, tile_weight, token_mask.reshape(1, tokens),
        tokens, 0,
    )
    total = summed_over(sums[0:1], "dp")
    return loss.reshape(tokens), total[0, 0] / total[0, 1]


def solution(mesh):
    in_specs = (P("dp", "vocab"), P("dp", "vocab"), P(), P("vocab", None, None, None), P("dp"))
    out_specs = (P("dp"), P())
    return jax.shard_map(local, mesh=mesh, in_specs=in_specs, out_specs=out_specs, check_vma=False)
```

```python
import functools

import jax
import jax.numpy as jnp
from jax import lax
from jax.experimental import pallas as pl
from jax.experimental.pallas import tpu as pltpu
from jax.sharding import PartitionSpec as P

BLOCK = 128
VS = 126976
K = 2
CAP = 3
SMOOTH = 0.1
LANES = 128
GROUP = 4
FACTS = 32
ROUTE = 24
F32 = jnp.float32
BF16 = jnp.bfloat16


def iota(shape, dim):
    return lax.broadcasted_iota(jnp.int32, shape, dim)


def selector(mask_row, rows, first):
    tokens = mask_row.shape[1]
    before = (iota((tokens, tokens), 0) < iota((tokens, tokens), 1)).astype(F32).astype(BF16)
    kept = jnp.broadcast_to(mask_row.astype(F32), (16, tokens)).astype(BF16)
    rank = jnp.dot(kept, before, preferred_element_type=F32)[0:1]
    wanted = (iota((rows, tokens), 0) + first).astype(F32)
    hit = (wanted == jnp.broadcast_to(rank, (rows, tokens))) & (
        jnp.broadcast_to(mask_row, (rows, tokens)) > 0
    )
    return hit.astype(F32).astype(BF16)


def thirds(value):
    high = value.astype(BF16).astype(F32)
    middle = (value - high).astype(BF16).astype(F32)
    low = (value - high - middle).astype(BF16).astype(F32)
    return high, middle, low


def in_lanes(columns, rows):
    lane = iota((rows, LANES), 1)
    out = jnp.zeros((rows, LANES), F32)
    for v, column in enumerate(columns):
        out = jnp.where(lane == v, jnp.broadcast_to(column, (rows, LANES)), out)
    return out


def column_copies(hbm, buf, sems, blocks, parts):
    groups = blocks // GROUP
    cuts = [groups * i // parts for i in range(parts + 1)]
    out = []
    for c, (lo, hi) in enumerate(zip(cuts[:-1], cuts[1:])):
        end = hi * GROUP if c < parts - 1 else blocks
        where = (slice(None), pl.ds(lo * GROUP * BLOCK, (end - lo * GROUP) * BLOCK))
        copy = pltpu.make_async_copy(hbm.at[where], buf.at[where], sems.at[c])
        copy.start()
        out.append(((lo, hi), copy))
    return out


def picked(sel_ref, src_ref, dst_ref, top_ref, blocks, copies):
    top_ref[...] = jnp.full(top_ref.shape, -jnp.inf, F32)

    def one(start, count):
        tops = []
        for i in range(0, count, 2):
            width = min(2, count - i) * BLOCK
            at = pl.ds(start + i * BLOCK, width)
            got = jnp.dot(sel_ref[...], src_ref[:, at], preferred_element_type=F32)
            dst_ref[:, at] = got.astype(BF16)
            tops += [got[:, j : j + BLOCK] for j in range(0, width, BLOCK)]
        top_ref[...] = functools.reduce(jnp.maximum, tops, top_ref[...])

    for (lo, hi), copy in copies:
        copy.wait()

        def body(i, carry):
            one(pl.multiple_of(i * GROUP * BLOCK, GROUP * BLOCK), GROUP)
            return carry

        lax.fori_loop(lo, hi, body, 0)
    if blocks % GROUP:
        one(blocks // GROUP * GROUP * BLOCK, blocks % GROUP)


def send_kernel(
    rows, first, sb_dev,
    me_ref, mask_ref, dest_hbm, x_hbm, w_hbm, s_hbm, send_hbm, kept_ref,
    x_buf, w_buf, s_buf, dest, sel, xc, maps, stage, cols, facts, top, total, used,
    in_sem, x_sem, s_sem, out_sem, fact_sem,
):
    blocks = w_buf.shape[0]
    s_blocks = s_buf.shape[1] // BLOCK
    peers = send_hbm.shape[0]
    w_copy = pltpu.make_async_copy(w_hbm, w_buf, in_sem.at[0])
    w_copy.start()
    dest_copy = pltpu.make_async_copy(dest_hbm, dest, in_sem.at[1])
    dest_copy.start()
    x_copies = column_copies(x_hbm, x_buf, x_sem, blocks, 3)
    s_copies = column_copies(s_hbm, s_buf, s_sem, s_blocks, 1)
    sel[...] = selector(mask_ref[...], rows, first)

    def clear(i, carry):
        used[i] = 0
        return carry

    lax.fori_loop(0, peers, clear, 0)
    w_copy.wait()
    ones = jnp.ones((K * BLOCK, BLOCK), BF16)

    def weight(b):
        both = jnp.concatenate([w_buf[b, k] for k in range(K)], axis=1)
        scale = 1.0 / jnp.dot(both, ones, preferred_element_type=F32)
        maps[b] = (both.astype(F32) * jnp.concatenate([scale] * K, axis=1)).astype(BF16)

    def weights(i, carry):
        for j in range(GROUP):
            weight(i * GROUP + j)
        return carry

    lax.fori_loop(0, blocks // GROUP, weights, 0)
    for b in range(blocks // GROUP * GROUP, blocks):
        weight(b)
    picked(sel, x_buf, xc, top, blocks, x_copies)
    highest = jnp.max(top[...], axis=1, keepdims=True)
    top[...] = jnp.broadcast_to(highest, top.shape)
    total[...] = jnp.zeros(total.shape, F32)
    dest_copy.wait()
    base = me_ref[0] * blocks
    top_block = peers * sb_dev
    factor = (1 << 16) // sb_dev + 1
    assert all(d * factor >> 16 == d // sb_dev for d in range(top_block))
    lane = iota((8, LANES), 1)

    def raised(b):
        at = pl.ds(pl.multiple_of(b * BLOCK, BLOCK), BLOCK)
        return jnp.exp(xc[:, at].astype(F32) - top[...])

    def tile(b, value, route):
        mapped = jnp.dot(value.astype(BF16), maps[b], preferred_element_type=F32)
        for k in range(K):
            stage[K * b + k] = mapped[:, k * BLOCK : (k + 1) * BLOCK].astype(BF16)
            block = dest[k, base + b]
            owner = lax.shift_right_logical(block * factor, 16)
            rank = used[owner]
            used[owner] = rank + 1
            near = (block - owner * sb_dev).astype(F32)
            route = jnp.where(lane == owner * CAP + rank, near, route)
            pltpu.make_async_copy(
                stage.at[K * b + k],
                send_hbm.at[owner, pl.ds(pl.multiple_of(rank * rows, 16), rows)],
                out_sem.at[K * b + k],
            ).start()
        return route

    def pair(i, route):
        one, two = raised(2 * i), raised(2 * i + 1)
        total[...] += one + two
        return tile(2 * i + 1, two, tile(2 * i, one, route))

    route = lax.fori_loop(0, blocks // 2, pair, jnp.full((8, LANES), sb_dev, F32))
    if blocks % 2:
        last = raised(blocks - 1)
        total[...] += last
        route = tile(blocks - 1, last, route)
    summed = jnp.sum(total[...], axis=1, keepdims=True)
    cols[...] = jnp.zeros(cols.shape, F32)

    picked(sel, s_buf, kept_ref, top, s_blocks, s_copies)
    s_highest = jnp.max(top[...], axis=1, keepdims=True)
    top[...] = jnp.broadcast_to(s_highest, top.shape)
    total[...] = jnp.zeros(total.shape, F32)

    def student(start, count):
        at = [pl.ds(start + i * BLOCK, BLOCK) for i in range(count)]
        total[...] += sum(jnp.exp(kept_ref[:, a].astype(F32) - top[...]) for a in at)

    def students(i, carry):
        student(pl.multiple_of(i * GROUP * BLOCK, GROUP * BLOCK), GROUP)
        return carry

    lax.fori_loop(0, s_blocks // GROUP, students, 0)
    if s_blocks % GROUP:
        student(s_blocks // GROUP * GROUP * BLOCK, s_blocks % GROUP)
    s_summed = jnp.sum(total[...], axis=1, keepdims=True)
    cols[0:rows] = in_lanes((highest, *thirds(summed), s_highest, *thirds(s_summed)), rows)
    for q in range(ROUTE // 8):
        if q < cols.shape[0] // LANES:
            turned = cols[q * LANES : (q + 1) * LANES].T
            total[q * 8 : (q + 1) * 8] = turned[:8]
        else:
            total[q * 8 : (q + 1) * 8] = jnp.zeros((8, LANES), F32)
    total[ROUTE : ROUTE + 8] = route
    facts[...] = total[0:FACTS].astype(BF16)

    def fact_copy(d):
        return pltpu.make_async_copy(
            facts, send_hbm.at[d, pl.ds(CAP * rows, FACTS)], fact_sem.at[d]
        )

    def fact_start(d, carry):
        fact_copy(d).start()
        return carry

    def fact_wait(d, carry):
        fact_copy(d).wait()
        return carry

    def tile_wait(i, carry):
        pltpu.make_async_copy(
            stage.at[i], send_hbm.at[0, pl.ds(0, rows)], out_sem.at[i]
        ).wait()
        return carry

    lax.fori_loop(0, peers, fact_start, 0)
    lax.fori_loop(0, K * blocks, tile_wait, 0)
    lax.fori_loop(0, peers, fact_wait, 0)


def combine_kernel(
    rows, first, chunk, everyone,
    me_ref, mask_ref, recv_hbm, s_ref, out_ref,
    buf, facts, facts32, share, near_vm, near, acc, cols, sems, fact_sem, near_sem,
):
    peers = recv_hbm.shape[0]
    blocks = s_ref.shape[1] // BLOCK
    spans = -(-rows // LANES)
    fact_copy = pltpu.make_async_copy(
        recv_hbm.at[:, pl.ds(CAP * rows, FACTS)], facts, fact_sem
    )
    fact_copy.start()

    def piece_copy(q, r):
        start = pl.multiple_of(q * chunk, chunk)
        return pltpu.make_async_copy(
            recv_hbm.at[:, pl.ds(r * rows + start, chunk)],
            buf.at[r, :, pl.ds(start, chunk)],
            sems.at[q, r],
        )

    for q in range(rows // chunk):
        for r in range(CAP):
            piece_copy(q, r).start()
    fact_copy.wait()
    facts32[...] = facts[...].astype(F32).reshape(facts32.shape)

    def fact(row):
        return facts32[pl.ds(row, peers, stride=FACTS), :]

    lane = iota((peers, LANES), 1)
    routes = fact(ROUTE)
    slots = jnp.zeros((peers, LANES), F32)
    for r in range(CAP):
        mine = jnp.where(lane == me_ref[0] * CAP + r, routes, 0.0)
        slots = jnp.where(lane == r, jnp.sum(mine, axis=1, keepdims=True), slots)
    near_vm[...] = slots.astype(jnp.int32)
    near_copy = pltpu.make_async_copy(near_vm, near, near_sem)
    near_copy.start()
    for q in range(spans):
        highest, high, middle, low, s_highest, s_high, s_middle, s_low = (
            fact(q * 8 + v) for v in range(8)
        )
        raised = jnp.exp(highest - jnp.max(highest, axis=0, keepdims=True))
        total = jnp.sum(raised * ((high + middle) + low), axis=0, keepdims=True)
        part = raised * ((1.0 - SMOOTH) / total)
        s_top = jnp.max(s_highest, axis=0, keepdims=True)
        s_total = jnp.sum(
            jnp.exp(s_highest - s_top) * ((s_high + s_middle) + s_low), axis=0, keepdims=True
        )
        norm = jnp.broadcast_to(s_top + jnp.log(s_total), (LANES - peers, LANES))
        share[q * LANES : (q + 1) * LANES] = jnp.concatenate([part, norm], axis=0).T
    cols[...] = jnp.zeros(cols.shape, F32)
    near_copy.wait()

    def work(q, carry):
        at = pl.ds(pl.multiple_of(q * chunk, chunk), chunk)
        shares = share[at]
        acc[...] = jnp.zeros(acc.shape, F32)
        for r in range(CAP):
            piece_copy(q, r).wait()
        for source in range(peers):
            scale = jnp.broadcast_to(shares[:, source : source + 1], (chunk, LANES))
            for r in range(CAP):
                acc[near[source, r]] += scale * buf[r, source, at].astype(F32)
        norm = jnp.broadcast_to(shares[:, peers : peers + 1], (chunk, LANES))

        def block(j, cross):
            target = acc[j] + SMOOTH / VS
            student = s_ref[at, pl.ds(pl.multiple_of(j * BLOCK, BLOCK), BLOCK)].astype(F32)
            return cross + target * (jnp.log(target) - (student - norm))

        cross = lax.fori_loop(0, blocks, block, jnp.zeros((chunk, LANES), F32))
        cols[at] = jnp.broadcast_to(jnp.sum(cross, axis=1, keepdims=True), (chunk, LANES))
        return carry

    lax.fori_loop(0, rows // chunk, work, 0)
    counted = jnp.sum(mask_ref[...].astype(F32), axis=1, keepdims=True)
    row = iota((8, LANES), 0)
    place = iota((8, LANES), 1)
    values = jnp.zeros((8, LANES), F32)
    part = jnp.zeros((8, LANES), F32)
    for q in range(spans):
        kl = cols[q * LANES : (q + 1) * LANES].T[:8]
        ahead = place + q * LANES
        kl = jnp.where((ahead < rows) & ((ahead + first).astype(F32) < counted), kl, 0.0)
        values = jnp.where(row % 4 == q, kl, values)
        part = part + kl
    whole_sum = jnp.broadcast_to(jnp.sum(part, axis=1, keepdims=True), (8, LANES))
    tally = jnp.where(place == 0, whole_sum, jnp.where(place == 1, counted, 0.0))
    values = jnp.where(row % 4 == 3, tally, values)
    for d in range(everyone // 2):
        out_ref[d * 8 : (d + 1) * 8] = values


def loss_kernel(rows, first, peers, group_ref, all_ref, mask_ref, loss_ref, sums_ref):
    everyone = all_ref.shape[0] // 4
    spans = -(-rows // LANES)
    base = group_ref[0] * (peers * 4)
    kl = jnp.concatenate(
        [
            jnp.sum(all_ref[pl.ds(base + q, peers, stride=4), :], axis=0, keepdims=True)
            for q in range(spans)
        ],
        axis=1,
    )
    mask = mask_ref[...]
    width = spans * LANES
    row = iota((16, width), 0)
    parts = jnp.zeros((16, width), F32)
    for v, part in enumerate(thirds(kl)):
        parts = jnp.where(row == v, jnp.broadcast_to(part, (16, width)), parts)
    back = jnp.dot(parts.astype(BF16), selector(mask, width, first), preferred_element_type=F32)
    loss_ref[...] = jnp.sum(back, axis=0, keepdims=True) * mask.astype(F32)
    tallies = all_ref[pl.ds(3, everyone, stride=4), :]
    lane = iota((1, LANES), 1)
    sums = jnp.sum(tallies, axis=0, keepdims=True)
    most = jnp.max(tallies, axis=0, keepdims=True)
    sums = jnp.where(lane == 1, sums * (1.0 / peers), sums)
    most = jnp.where(lane == 1, most, 0.0)
    row = iota((8, LANES), 0)
    sums_ref[...] = jnp.where(
        row == 0, jnp.broadcast_to(sums, (8, LANES)), jnp.broadcast_to(most, (8, LANES))
    )


def whole(memory_space):
    return pl.BlockSpec(memory_space=memory_space)


VM, SM, HB = pltpu.VMEM, pltpu.SMEM, pltpu.HBM


def exchanged(teacher_logits, student_logits, dest, tile_weight, mask, rows, first):
    peers = lax.axis_size("vocab")
    everyone = peers * lax.axis_size("dp")
    me = lax.axis_index("vocab").astype(jnp.int32).reshape(1)
    group = lax.axis_index("dp").astype(jnp.int32).reshape(1)
    tokens = teacher_logits.shape[0]
    tb_dev = teacher_logits.shape[1] // BLOCK
    sb_dev = student_logits.shape[1] // BLOCK
    wide = -(-rows // LANES) * LANES
    tiles = tb_dev * K
    dma = pltpu.SemaphoreType.DMA
    tall = max(rows, LANES)
    send, kept = pl.pallas_call(
        functools.partial(send_kernel, rows, first, sb_dev),
        out_shape=(
            jax.ShapeDtypeStruct((peers, CAP * rows + FACTS, LANES), BF16),
            jax.ShapeDtypeStruct((rows, student_logits.shape[1]), BF16),
        ),
        in_specs=[whole(SM), whole(VM), whole(HB), whole(HB), whole(HB), whole(HB)],
        out_specs=(whole(HB), whole(VM)),
        scratch_shapes=[
            VM(teacher_logits.shape, BF16),
            VM(tile_weight.shape, BF16),
            VM(student_logits.shape, BF16),
            SM(dest.shape, jnp.int32),
            VM((rows, tokens), BF16),
            VM((rows, tb_dev * BLOCK), BF16),
            VM((tb_dev, BLOCK, K * BLOCK), BF16),
            VM((tiles, rows, BLOCK), BF16),
            VM((wide, LANES), F32),
            VM((FACTS, LANES), BF16),
            VM((rows, LANES), F32),
            VM((rows, LANES), F32),
            SM((peers,), jnp.int32),
            dma((2,)),
            dma((3,)),
            dma((1,)),
            dma((tiles,)),
            dma((peers,)),
        ],
        compiler_params=pltpu.CompilerParams(vmem_limit_bytes=56 << 20),
        name="send",
    )(me, mask, dest, teacher_logits, tile_weight, student_logits)
    received = lax.all_to_all(send, "vocab", 0, 0, tiled=True)
    chunk = rows // 4 if rows % 64 == 0 else rows
    mine = pl.pallas_call(
        functools.partial(combine_kernel, rows, first, chunk, everyone),
        out_shape=jax.ShapeDtypeStruct((everyone * 4, LANES), F32),
        in_specs=[whole(SM), whole(VM), whole(HB), whole(VM)],
        out_specs=whole(VM),
        scratch_shapes=[
            VM((CAP, peers, rows, LANES), BF16),
            VM((peers, FACTS, LANES), BF16),
            VM((peers * FACTS, LANES), F32),
            VM((wide, LANES), F32),
            VM((peers, LANES), jnp.int32),
            SM((peers, LANES), jnp.int32),
            VM((sb_dev + 1, chunk, LANES), F32),
            VM((wide, LANES), F32),
            dma((rows // chunk, CAP)),
            dma(()),
            dma(()),
        ],
        compiler_params=pltpu.CompilerParams(vmem_limit_bytes=40 << 20),
        name="combine",
    )(me, mask, received, kept)
    collected = lax.all_to_all(mine, ("dp", "vocab"), 0, 0, tiled=True)
    return pl.pallas_call(
        functools.partial(loss_kernel, rows, first, peers),
        out_shape=(
            jax.ShapeDtypeStruct((1, tokens), F32),
            jax.ShapeDtypeStruct((8, LANES), F32),
        ),
        in_specs=[whole(SM), whole(VM), whole(VM)],
        out_specs=(whole(VM), whole(VM)),
        name="loss",
    )(group, collected, mask)


def local(teacher_logits, student_logits, tile_dest, tile_weight, token_mask):
    tokens = teacher_logits.shape[0]
    mask = token_mask.reshape(1, tokens)
    parts = (teacher_logits, student_logits, tile_dest.T, tile_weight, mask)
    rows = tokens * 5 // 6 if tokens % 384 == 0 else tokens
    loss, sums = exchanged(*parts, rows, 0)
    total = sums[0, 0]
    if rows < tokens:

        def rest():
            more, more_sums = exchanged(*parts, tokens - rows, rows)
            return loss + more, total + more_sums[0, 0]

        loss, total = lax.cond(sums[1, 1] > rows, rest, lambda: (loss, total))
    return loss.reshape(tokens), total / sums[0, 1]


def solution(mesh):
    in_specs = (P("dp", "vocab"), P("dp", "vocab"), P(), P("vocab", None, None, None), P("dp"))
    out_specs = (P("dp"), P())
    return jax.shard_map(local, mesh=mesh, in_specs=in_specs, out_specs=out_specs, check_vma=False)
```

```python
import functools

import jax
import jax.numpy as jnp
from jax import lax
from jax.experimental import pallas as pl
from jax.experimental.pallas import tpu as pltpu
from jax.sharding import PartitionSpec as P

BLOCK = 128
VS = 126976
K = 2
CAP = 3
SMOOTH = 0.1
LANES = 128
GROUP = 4
FACTS = 16
ROUTE = 15
VALUES = 6
F32 = jnp.float32
BF16 = jnp.bfloat16


def iota(shape, dim):
    return lax.broadcasted_iota(jnp.int32, shape, dim)


def selector(mask_row, rows, first):
    tokens = mask_row.shape[1]
    before = (iota((tokens, tokens), 0) < iota((tokens, tokens), 1)).astype(F32).astype(BF16)
    kept = jnp.broadcast_to(mask_row.astype(F32), (16, tokens)).astype(BF16)
    rank = jnp.dot(kept, before, preferred_element_type=F32)[0:1]
    wanted = (iota((rows, tokens), 0) + first).astype(F32)
    hit = (wanted == jnp.broadcast_to(rank, (rows, tokens))) & (
        jnp.broadcast_to(mask_row, (rows, tokens)) > 0
    )
    return hit.astype(F32).astype(BF16)


def parted(value, count):
    out = []
    for _ in range(count):
        out.append(value.astype(BF16).astype(F32))
        value = value - out[-1]
    return out


def in_lanes(columns, rows):
    lane = iota((rows, LANES), 1)
    out = jnp.zeros((rows, LANES), F32)
    for v, column in enumerate(columns):
        out = jnp.where(lane == v, jnp.broadcast_to(column, (rows, LANES)), out)
    return out


def column_copies(hbm, buf, sems, blocks, parts):
    groups = blocks // GROUP
    cuts = [groups * i // parts for i in range(parts + 1)]
    out = []
    for c, (lo, hi) in enumerate(zip(cuts[:-1], cuts[1:])):
        end = hi * GROUP if c < parts - 1 else blocks
        where = (slice(None), pl.ds(lo * GROUP * BLOCK, (end - lo * GROUP) * BLOCK))
        copy = pltpu.make_async_copy(hbm.at[where], buf.at[where], sems.at[c])
        copy.start()
        out.append(((lo, hi), copy))
    return out


def picked(sel_ref, src_ref, dst_ref, top_ref, start, count):
    tops = []
    for i in range(0, count, 2):
        width = min(2, count - i) * BLOCK
        at = pl.ds(start + i * BLOCK, width)
        got = jnp.dot(sel_ref[...], src_ref[:, at], preferred_element_type=F32)
        dst_ref[:, at] = got.astype(BF16)
        tops += [got[:, j : j + BLOCK] for j in range(0, width, BLOCK)]
    top_ref[...] = functools.reduce(jnp.maximum, tops, top_ref[...])


def send_kernel(
    rows, first, sb_dev,
    me_ref, mask_ref, dest_hbm, x_hbm, w_hbm, s_hbm, send_hbm, kept_hbm,
    x_buf, w_buf, s_buf, dest, sel, xc, kept, maps, stage, cols, facts,
    top, total, s_top, s_total, used,
    in_sem, x_sem, s_sem, kept_sem, out_sem, fact_sem,
):
    blocks = w_buf.shape[0]
    s_blocks = s_buf.shape[1] // BLOCK
    peers = send_hbm.shape[0]
    w_copy = pltpu.make_async_copy(w_hbm, w_buf, in_sem.at[0])
    w_copy.start()
    x_copies = column_copies(x_hbm, x_buf, x_sem, blocks, 3)
    ((_, s_copy),) = column_copies(s_hbm, s_buf, s_sem, s_blocks, 1)
    dest_copy = pltpu.make_async_copy(dest_hbm, dest, in_sem.at[1])
    dest_copy.start()
    sel[...] = selector(mask_ref[...].reshape(1, -1), rows, first)
    top[...] = jnp.full(top.shape, -jnp.inf, F32)
    s_top[...] = jnp.full(top.shape, -jnp.inf, F32)
    total[...] = jnp.zeros(total.shape, F32)
    s_total[...] = jnp.zeros(total.shape, F32)

    def clear(i, carry):
        used[i] = 0
        return carry

    lax.fori_loop(0, peers, clear, 0)
    w_copy.wait()
    ones = jnp.ones((K * BLOCK, BLOCK), BF16)

    def weight(b):
        both = jnp.concatenate([w_buf[b, k] for k in range(K)], axis=1)
        scale = 1.0 / jnp.dot(both, ones, preferred_element_type=F32)
        maps[b] = (both.astype(F32) * jnp.concatenate([scale] * K, axis=1)).astype(BF16)

    def teacher(i, count):
        start = i * GROUP * BLOCK
        if not isinstance(i, int):
            start = pl.multiple_of(start, GROUP * BLOCK)
        picked(sel, x_buf, xc, top, start, count)
        for j in range(count):
            weight(i * GROUP + j)

    def teachers(i, carry):
        teacher(i, GROUP)
        return carry

    for (lo, hi), copy in x_copies:
        copy.wait()
        lax.fori_loop(lo, hi, teachers, 0)
    if blocks % GROUP:
        teacher(blocks // GROUP, blocks % GROUP)
    highest = jnp.max(top[...], axis=1, keepdims=True)
    top[...] = jnp.broadcast_to(highest, top.shape)
    dest_copy.wait()
    s_copy.wait()
    base = me_ref[0] * blocks
    factor = (1 << 16) // sb_dev + 1
    assert all(d * factor >> 16 == d // sb_dev for d in range(peers * sb_dev))
    lane = iota((8, LANES), 1)

    def raised(b):
        at = pl.ds(pl.multiple_of(b * BLOCK, BLOCK), BLOCK)
        return jnp.exp(xc[:, at].astype(F32) - top[...])

    def tile(b, value, route):
        mapped = jnp.dot(value.astype(BF16), maps[b], preferred_element_type=F32)
        for k in range(K):
            stage[K * b + k] = mapped[:, k * BLOCK : (k + 1) * BLOCK].astype(BF16)
            block = dest[k, base + b]
            owner = lax.shift_right_logical(block * factor, 16)
            rank = used[owner]
            used[owner] = rank + 1
            near = (block - owner * sb_dev).astype(F32)
            route = jnp.where(lane == owner * CAP + rank, near, route)
            pltpu.make_async_copy(
                stage.at[K * b + k],
                send_hbm.at[owner, pl.ds(pl.multiple_of(rank * rows, 16), rows)],
                out_sem,
            ).start()
        return route

    def pair(i, route):
        one, two = raised(2 * i), raised(2 * i + 1)
        total[...] += one + two
        return tile(2 * i + 1, two, tile(2 * i, one, route))

    def both(i, route):
        picked(sel, s_buf, kept, s_top, pl.multiple_of(i * 2 * BLOCK, 2 * BLOCK), 2)
        return pair(i, route)

    shared = min(blocks, s_blocks) // 2
    route = lax.fori_loop(0, shared, both, jnp.full((8, LANES), sb_dev, F32))
    for i in range(shared, blocks // 2):
        route = pair(i, route)
    for b in range(2 * shared, s_blocks, 2):
        picked(sel, s_buf, kept, s_top, b * BLOCK, min(2, s_blocks - b))
    kept_copy = pltpu.make_async_copy(kept, kept_hbm, kept_sem)
    kept_copy.start()
    if blocks % 2:
        last = raised(blocks - 1)
        total[...] += last
        route = tile(blocks - 1, last, route)
    summed = jnp.sum(total[...], axis=1, keepdims=True)
    s_highest = jnp.max(s_top[...], axis=1, keepdims=True)
    s_top[...] = jnp.broadcast_to(s_highest, top.shape)

    def student(start, count):
        at = [pl.ds(start + i * BLOCK, BLOCK) for i in range(count)]
        s_total[...] += sum(jnp.exp(kept[:, a].astype(F32) - s_top[...]) for a in at)

    def students(i, carry):
        student(pl.multiple_of(i * GROUP * BLOCK, GROUP * BLOCK), GROUP)
        return carry

    lax.fori_loop(0, s_blocks // GROUP, students, 0)
    if s_blocks % GROUP:
        student(s_blocks // GROUP * GROUP * BLOCK, s_blocks % GROUP)
    s_summed = jnp.sum(s_total[...], axis=1, keepdims=True)
    columns = (highest, *parted(summed, 2), s_highest, *parted(s_summed, 2))
    full = rows // LANES
    rest = rows - full * LANES
    cols[...] = jnp.zeros(cols.shape, F32)
    cols[0:rows] = in_lanes(columns, rows)
    if rest:
        upper = [column[full * LANES :] for column in columns[VALUES // 2 :]]
        cols[full * LANES + LANES // 2 : full * LANES + LANES // 2 + rest] = in_lanes(upper, rest)
    total[0:FACTS] = jnp.zeros((FACTS, LANES), F32)
    for q in range(full + (rest > 0)):
        turned = cols[q * LANES : (q + 1) * LANES].T
        height = VALUES if q < full else VALUES // 2
        total[q * VALUES : q * VALUES + height] = turned[:height]
    total[ROUTE : ROUTE + 1] = route[0:1]
    facts[...] = jnp.broadcast_to(total[0:FACTS].astype(BF16)[None], facts.shape)
    fact_copy = pltpu.make_async_copy(
        facts, send_hbm.at[:, pl.ds(CAP * rows, FACTS)], fact_sem
    )
    fact_copy.start()
    pltpu.make_async_copy(stage, stage, out_sem).wait()
    kept_copy.wait()
    fact_copy.wait()


def combine_kernel(
    rows, first, chunk,
    me_ref, mask_ref, recv_hbm, s_ref, out_ref,
    buf, facts, facts32, share, near_vm, near, acc, cols, sems, fact_sem, near_sem,
):
    peers = recv_hbm.shape[0]
    blocks = s_ref.shape[1] // BLOCK
    spans = -(-rows // LANES)
    fact_copy = pltpu.make_async_copy(
        recv_hbm.at[:, pl.ds(CAP * rows, FACTS)], facts, fact_sem
    )
    fact_copy.start()

    def piece_copy(q, r):
        start = pl.multiple_of(q * chunk, chunk)
        return pltpu.make_async_copy(
            recv_hbm.at[:, pl.ds(r * rows + start, chunk)],
            buf.at[r, :, pl.ds(start, chunk)],
            sems.at[q, r],
        )

    for q in range(rows // chunk):
        for r in range(CAP):
            piece_copy(q, r).start()
    fact_copy.wait()
    facts32[...] = facts[...].astype(F32).reshape(facts32.shape)

    def fact(row):
        return facts32[pl.ds(row, peers, stride=FACTS), :]

    lane = iota((peers, LANES), 1)
    routes = fact(ROUTE)
    slots = jnp.zeros((peers, LANES), F32)
    for r in range(CAP):
        mine = jnp.where(lane == me_ref[0] * CAP + r, routes, 0.0)
        slots = jnp.where(lane == r, jnp.sum(mine, axis=1, keepdims=True), slots)
    near_vm[...] = slots.astype(jnp.int32)
    near_copy = pltpu.make_async_copy(near_vm, near, near_sem)
    near_copy.start()
    for q in range(spans):
        if (q + 1) * LANES <= rows:
            values = [fact(q * VALUES + v) for v in range(VALUES)]
        else:
            values = [fact(q * VALUES + v) for v in range(VALUES // 2)]
            values += [pltpu.roll(value, LANES // 2, 1) for value in values]
        highest, high, low, s_highest, s_high, s_low = values
        raised = jnp.exp(highest - jnp.max(highest, axis=0, keepdims=True))
        total = jnp.sum(raised * (high + low), axis=0, keepdims=True)
        part = raised * ((1.0 - SMOOTH) / total)
        s_top = jnp.max(s_highest, axis=0, keepdims=True)
        s_total = jnp.sum(jnp.exp(s_highest - s_top) * (s_high + s_low), axis=0, keepdims=True)
        norm = jnp.broadcast_to(s_top + jnp.log(s_total), (LANES - peers, LANES))
        share[q * LANES : (q + 1) * LANES] = jnp.concatenate([part, norm], axis=0).T
    cols[...] = jnp.zeros(cols.shape, F32)
    near_copy.wait()

    def work(q, carry):
        at = pl.ds(pl.multiple_of(q * chunk, chunk), chunk)
        shares = share[at]
        acc[...] = jnp.zeros(acc.shape, F32)
        for r in range(CAP):
            piece_copy(q, r).wait()
        for source in range(peers):
            scale = jnp.broadcast_to(shares[:, source : source + 1], (chunk, LANES))
            for r in range(CAP):
                acc[near[source, r]] += scale * buf[r, source, at].astype(F32)
        norm = jnp.broadcast_to(shares[:, peers : peers + 1], (chunk, LANES))

        def block(j, cross):
            target = acc[j] + SMOOTH / VS
            student = s_ref[at, pl.ds(pl.multiple_of(j * BLOCK, BLOCK), BLOCK)].astype(F32)
            return cross + target * (jnp.log(target) - (student - norm))

        cross = lax.fori_loop(0, blocks, block, jnp.zeros((chunk, LANES), F32))
        cols[at] = jnp.broadcast_to(jnp.sum(cross, axis=1, keepdims=True), (chunk, LANES))
        return carry

    lax.fori_loop(0, rows // chunk, work, 0)
    counted = jnp.sum(mask_ref[...].reshape(1, -1).astype(F32), axis=1, keepdims=True)
    row = iota((8, LANES), 0)
    place = iota((8, LANES), 1)
    values = jnp.zeros((8, LANES), F32)
    part = jnp.zeros((8, LANES), F32)
    for q in range(spans):
        kl = cols[q * LANES : (q + 1) * LANES].T[:8]
        ahead = place + q * LANES
        kl = jnp.where((ahead < rows) & ((ahead + first).astype(F32) < counted), kl, 0.0)
        values = jnp.where(row % 4 == q, kl, values)
        part = part + kl
    whole_sum = jnp.broadcast_to(jnp.sum(part, axis=1, keepdims=True), (8, LANES))
    tally = jnp.where(place == 0, whole_sum, jnp.where(place == 1, counted, 0.0))
    values = jnp.where(row % 4 == 3, tally, values)
    for d in range(peers // 2):
        out_ref[d * 8 : (d + 1) * 8] = values


def tally_kernel(all_ref, out_ref):
    peers = all_ref.shape[0] // 4
    sums = jnp.sum(all_ref[pl.ds(3, peers, stride=4), :], axis=0, keepdims=True)
    lane = iota((1, LANES), 1)
    sums = jnp.where(lane == 1, sums * (1.0 / peers), sums)
    out_ref[...] = jnp.broadcast_to(sums, out_ref.shape)


def loss_kernel(rows, first, all_ref, mask_ref, loss_ref):
    peers = all_ref.shape[0] // 4
    spans = -(-rows // LANES)
    kl = jnp.concatenate(
        [
            jnp.sum(all_ref[pl.ds(q, peers, stride=4), :], axis=0, keepdims=True)
            for q in range(spans)
        ],
        axis=1,
    )
    mask = mask_ref[...].reshape(1, -1)
    width = spans * LANES
    row = iota((16, width), 0)
    parts = jnp.zeros((16, width), F32)
    for v, part in enumerate(parted(kl, 3)):
        parts = jnp.where(row == v, jnp.broadcast_to(part, (16, width)), parts)
    back = jnp.dot(parts.astype(BF16), selector(mask, width, first), preferred_element_type=F32)
    loss = jnp.sum(back, axis=0, keepdims=True) * mask.astype(F32)
    loss_ref[...] = loss.reshape(loss_ref.shape)


def close_kernel(rows, tally_ref, mean_ref, over_ref):
    lane = iota((1, LANES), 1)
    sums = jnp.sum(tally_ref[...], axis=0, keepdims=True)
    most = jnp.max(tally_ref[...], axis=0, keepdims=True)
    total = jnp.sum(jnp.where(lane == 0, sums, 0.0), axis=1, keepdims=True)
    count = jnp.sum(jnp.where(lane == 1, sums, 0.0), axis=1, keepdims=True)
    mean_ref[0] = jnp.sum(total / count)
    over_ref[0] = jnp.max(jnp.where((lane == 1) & (most > rows), 1, 0))


def whole(memory_space):
    return pl.BlockSpec(memory_space=memory_space)


VM, SM, HB = pltpu.VMEM, pltpu.SMEM, pltpu.HBM
SMALL = pltpu.CompilerParams(vmem_limit_bytes=6 << 20)


def exchanged(teacher_logits, student_logits, dest, tile_weight, mask, rows, first):
    peers = lax.axis_size("vocab")
    groups = lax.axis_size("dp")
    me = lax.axis_index("vocab").astype(jnp.int32).reshape(1)
    tokens = teacher_logits.shape[0]
    tb_dev = teacher_logits.shape[1] // BLOCK
    sb_dev = student_logits.shape[1] // BLOCK
    wide = -(-rows // LANES) * LANES
    tiles = tb_dev * K
    dma = pltpu.SemaphoreType.DMA
    tall = max(rows, LANES)
    send, kept = pl.pallas_call(
        functools.partial(send_kernel, rows, first, sb_dev),
        out_shape=(
            jax.ShapeDtypeStruct((peers, CAP * rows + FACTS, LANES), BF16),
            jax.ShapeDtypeStruct((rows, student_logits.shape[1]), BF16),
        ),
        in_specs=[whole(SM), whole(VM), whole(HB), whole(HB), whole(HB), whole(HB)],
        out_specs=(whole(HB), whole(HB)),
        scratch_shapes=[
            VM(teacher_logits.shape, BF16),
            VM(tile_weight.shape, BF16),
            VM(student_logits.shape, BF16),
            SM(dest.shape, jnp.int32),
            VM((rows, tokens), BF16),
            VM((rows, tb_dev * BLOCK), BF16),
            VM((rows, sb_dev * BLOCK), BF16),
            VM((tb_dev, BLOCK, K * BLOCK), BF16),
            VM((tiles, rows, BLOCK), BF16),
            VM((wide, LANES), F32),
            VM((peers, FACTS, LANES), BF16),
            VM((rows, LANES), F32),
            VM((rows, LANES), F32),
            VM((rows, LANES), F32),
            VM((rows, LANES), F32),
            SM((peers,), jnp.int32),
            dma((2,)),
            dma((3,)),
            dma((1,)),
            dma(()),
            dma(()),
            dma(()),
        ],
        compiler_params=pltpu.CompilerParams(vmem_limit_bytes=56 << 20),
        name="send",
    )(me, mask, dest, teacher_logits, tile_weight, student_logits)
    received = lax.all_to_all(send, "vocab", 0, 0, tiled=True)
    chunk = rows // 4 if rows % 64 == 0 else rows
    mine = pl.pallas_call(
        functools.partial(combine_kernel, rows, first, chunk),
        out_shape=jax.ShapeDtypeStruct((peers * 4, LANES), F32),
        in_specs=[whole(SM), whole(VM), whole(HB), whole(VM)],
        out_specs=whole(VM),
        scratch_shapes=[
            VM((CAP, peers, rows, LANES), BF16),
            VM((peers, FACTS, LANES), BF16),
            VM((peers * FACTS, LANES), F32),
            VM((wide, LANES), F32),
            VM((peers, LANES), jnp.int32),
            SM((peers, LANES), jnp.int32),
            VM((sb_dev + 1, chunk, LANES), F32),
            VM((wide, LANES), F32),
            dma((rows // chunk, CAP)),
            dma(()),
            dma(()),
        ],
        compiler_params=pltpu.CompilerParams(vmem_limit_bytes=40 << 20),
        name="combine",
    )(me, mask, received, kept)
    collected = lax.all_to_all(mine, "vocab", 0, 0, tiled=True)
    tally = pl.pallas_call(
        tally_kernel,
        out_shape=jax.ShapeDtypeStruct((groups, LANES), F32),
        in_specs=[whole(VM)],
        out_specs=whole(VM),
        compiler_params=SMALL,
        name="tally",
    )(collected)
    tally = lax.all_to_all(tally, "dp", 0, 0, tiled=True)
    loss = pl.pallas_call(
        functools.partial(loss_kernel, rows, first),
        out_shape=jax.ShapeDtypeStruct((tokens,), F32),
        in_specs=[whole(VM), whole(VM)],
        out_specs=whole(VM),
        cost_estimate=pl.CostEstimate(flops=10**10, bytes_accessed=10**6, transcendentals=0),
        compiler_params=SMALL,
        name="loss",
    )(collected, mask)
    mean, over = pl.pallas_call(
        functools.partial(close_kernel, rows),
        out_shape=(jax.ShapeDtypeStruct((1,), F32), jax.ShapeDtypeStruct((1,), jnp.int32)),
        in_specs=[whole(VM)],
        out_specs=(whole(SM), whole(SM)),
        compiler_params=SMALL,
        name="close",
    )(tally)
    return loss, mean.reshape(()), over.reshape(())


def local(teacher_logits, student_logits, tile_dest, tile_weight, token_mask):
    tokens = teacher_logits.shape[0]
    parts = (teacher_logits, student_logits, tile_dest.T, tile_weight, token_mask)
    rows = tokens * 5 // 6 if tokens % 384 == 0 else tokens
    loss, mean, over = exchanged(*parts, rows, 0)
    if rows < tokens:

        def rest():
            more, more_mean, _ = exchanged(*parts, tokens - rows, rows)
            return loss + more, mean + more_mean

        loss, mean = lax.cond(over > 0, rest, lambda: (loss, mean))
    return loss, mean


def solution(mesh):
    in_specs = (P("dp", "vocab"), P("dp", "vocab"), P(), P("vocab", None, None, None), P("dp"))
    out_specs = (P("dp"), P())
    return jax.shard_map(local, mesh=mesh, in_specs=in_specs, out_specs=out_specs, check_vma=False)
```

```python
import functools

import jax
import jax.numpy as jnp
from jax import lax
from jax.experimental import pallas as pl
from jax.experimental.pallas import tpu as pltpu
from jax.sharding import PartitionSpec as P

BLOCK = 128
VS = 126976
K = 2
CAP = 3
SMOOTH = 0.1
LANES = 128
GROUP = 8
FACTS = 16
ROUTE = 15
VALUES = 6
F32 = jnp.float32
BF16 = jnp.bfloat16


def iota(shape, dim):
    return lax.broadcasted_iota(jnp.int32, shape, dim)


def selector(mask_row, rows, first):
    tokens = mask_row.shape[1]
    before = (iota((tokens, tokens), 0) < iota((tokens, tokens), 1)).astype(F32).astype(BF16)
    kept = jnp.broadcast_to(mask_row.astype(F32), (16, tokens)).astype(BF16)
    rank = jnp.dot(kept, before, preferred_element_type=F32)[0:1]
    wanted = (iota((rows, tokens), 0) + first).astype(F32)
    hit = (wanted == jnp.broadcast_to(rank, (rows, tokens))) & (
        jnp.broadcast_to(mask_row, (rows, tokens)) > 0
    )
    return hit.astype(F32).astype(BF16)


def parted(value, count):
    out = []
    for _ in range(count):
        out.append(value.astype(BF16).astype(F32))
        value = value - out[-1]
    return out


def in_lanes(columns, rows):
    lane = iota((rows, LANES), 1)
    out = jnp.zeros((rows, LANES), F32)
    for v, column in enumerate(columns):
        out = jnp.where(lane == v, jnp.broadcast_to(column, (rows, LANES)), out)
    return out


def column_copies(hbm, buf, sems, blocks, parts):
    groups = blocks // GROUP
    cuts = [groups * i // parts for i in range(parts + 1)]
    out = []
    for c, (lo, hi) in enumerate(zip(cuts[:-1], cuts[1:])):
        end = hi * GROUP if c < parts - 1 else blocks
        where = (slice(None), pl.ds(lo * GROUP * BLOCK, (end - lo * GROUP) * BLOCK))
        copy = pltpu.make_async_copy(hbm.at[where], buf.at[where], sems.at[c])
        copy.start()
        out.append(((lo, hi), copy))
    return out


def picked(sel_ref, src_ref, dst_ref, top_ref, start, count):
    tops = []
    for i in range(0, count, 2):
        width = min(2, count - i) * BLOCK
        at = pl.ds(start + i * BLOCK, width)
        got = jnp.dot(sel_ref[...], src_ref[:, at], preferred_element_type=F32)
        dst_ref[:, at] = got.astype(BF16)
        tops += [got[:, j : j + BLOCK] for j in range(0, width, BLOCK)]
    top_ref[...] = functools.reduce(jnp.maximum, tops, top_ref[...])


def send_kernel(
    rows, first, sb_dev,
    me_ref, mask_ref, dest_hbm, x_hbm, w_hbm, s_hbm, send_ref, kept,
    x_buf, w_buf, s_buf, dest, sel, xc, maps, cols,
    top, total, s_top, s_total, used,
    in_sem, x_sem, s_sem,
):
    blocks = w_buf.shape[0]
    s_blocks = s_buf.shape[1] // BLOCK
    peers = send_ref.shape[0]
    w_copy = pltpu.make_async_copy(w_hbm, w_buf, in_sem.at[0])
    w_copy.start()
    x_copies = column_copies(x_hbm, x_buf, x_sem, blocks, 3)
    ((_, s_copy),) = column_copies(s_hbm, s_buf, s_sem, s_blocks, 1)
    dest_copy = pltpu.make_async_copy(dest_hbm, dest, in_sem.at[1])
    dest_copy.start()
    sel[...] = selector(mask_ref[...].reshape(1, -1), rows, first)
    top[...] = jnp.full(top.shape, -jnp.inf, F32)
    s_top[...] = jnp.full(top.shape, -jnp.inf, F32)
    total[...] = jnp.zeros(total.shape, F32)
    s_total[...] = jnp.zeros(total.shape, F32)

    def clear(i, carry):
        used[i] = 0
        return carry

    lax.fori_loop(0, peers, clear, 0)
    w_copy.wait()
    ones = jnp.ones((K * BLOCK, BLOCK), BF16)

    def weight(b):
        both = jnp.concatenate([w_buf[b, k] for k in range(K)], axis=1)
        scale = 1.0 / jnp.dot(both, ones, preferred_element_type=F32)
        maps[b] = (both.astype(F32) * jnp.concatenate([scale] * K, axis=1)).astype(BF16)

    def teacher(i, count):
        start = i * GROUP * BLOCK
        if not isinstance(i, int):
            start = pl.multiple_of(start, GROUP * BLOCK)
        picked(sel, x_buf, xc, top, start, count)
        for j in range(count):
            weight(i * GROUP + j)

    def teachers(i, carry):
        teacher(i, GROUP)
        return carry

    for (lo, hi), copy in x_copies:
        copy.wait()
        lax.fori_loop(lo, hi, teachers, 0)
    if blocks % GROUP:
        teacher(blocks // GROUP, blocks % GROUP)
    highest = jnp.max(top[...], axis=1, keepdims=True)
    top[...] = jnp.broadcast_to(highest, top.shape)
    dest_copy.wait()
    s_copy.wait()
    base = me_ref[0] * blocks
    factor = (1 << 16) // sb_dev + 1
    assert all(d * factor >> 16 == d // sb_dev for d in range(peers * sb_dev))
    lane = iota((8, LANES), 1)

    def raised(b):
        at = pl.ds(pl.multiple_of(b * BLOCK, BLOCK), BLOCK)
        return jnp.exp(xc[:, at].astype(F32) - top[...])

    def tile(b, value, route):
        mapped = jnp.dot(value.astype(BF16), maps[b], preferred_element_type=F32)
        for k in range(K):
            block = dest[k, base + b]
            owner = lax.shift_right_logical(block * factor, 16)
            rank = used[owner]
            used[owner] = rank + 1
            near = (block - owner * sb_dev).astype(F32)
            route = jnp.where(lane == owner * CAP + rank, near, route)
            at = pl.ds(pl.multiple_of(rank * rows, 16), rows)
            send_ref[owner, at] = mapped[:, k * BLOCK : (k + 1) * BLOCK].astype(BF16)
        return route

    def pair(i, route):
        one, two = raised(2 * i), raised(2 * i + 1)
        total[...] += one + two
        return tile(2 * i + 1, two, tile(2 * i, one, route))

    def both(i, route):
        picked(sel, s_buf, kept, s_top, pl.multiple_of(i * 4 * BLOCK, 4 * BLOCK), 4)
        return pair(2 * i + 1, pair(2 * i, route))

    shared = min(blocks, s_blocks) // 4 * 2
    route = lax.fori_loop(0, shared // 2, both, jnp.full((8, LANES), sb_dev, F32))
    for i in range(shared, blocks // 2):
        route = pair(i, route)
    for b in range(2 * shared, s_blocks, 2):
        picked(sel, s_buf, kept, s_top, b * BLOCK, min(2, s_blocks - b))
    if blocks % 2:
        last = raised(blocks - 1)
        total[...] += last
        route = tile(blocks - 1, last, route)
    summed = jnp.sum(total[...], axis=1, keepdims=True)
    s_highest = jnp.max(s_top[...], axis=1, keepdims=True)
    s_top[...] = jnp.broadcast_to(s_highest, top.shape)

    def student(start, count):
        at = [pl.ds(start + i * BLOCK, BLOCK) for i in range(count)]
        s_total[...] += sum(jnp.exp(kept[:, a].astype(F32) - s_top[...]) for a in at)

    def students(i, carry):
        student(pl.multiple_of(i * GROUP * BLOCK, GROUP * BLOCK), GROUP)
        return carry

    lax.fori_loop(0, s_blocks // GROUP, students, 0)
    if s_blocks % GROUP:
        student(s_blocks // GROUP * GROUP * BLOCK, s_blocks % GROUP)
    s_summed = jnp.sum(s_total[...], axis=1, keepdims=True)
    columns = (highest, *parted(summed, 2), s_highest, *parted(s_summed, 2))
    full = rows // LANES
    rest = rows - full * LANES
    cols[...] = jnp.zeros(cols.shape, F32)
    cols[0:rows] = in_lanes(columns, rows)
    if rest:
        upper = [column[full * LANES :] for column in columns[VALUES // 2 :]]
        cols[full * LANES + LANES // 2 : full * LANES + LANES // 2 + rest] = in_lanes(upper, rest)
    total[0:FACTS] = jnp.zeros((FACTS, LANES), F32)
    for q in range(full + (rest > 0)):
        turned = cols[q * LANES : (q + 1) * LANES].T
        height = VALUES if q < full else VALUES // 2
        total[q * VALUES : q * VALUES + height] = turned[:height]
    total[ROUTE : ROUTE + 1] = route[0:1]
    facts = total[0:FACTS].astype(BF16)
    for d in range(peers):
        send_ref[d, CAP * rows : CAP * rows + FACTS] = facts


def combine_kernel(
    rows, first, chunk,
    me_ref, mask_ref, recv_ref, s_ref, out_ref,
    facts32, share, near_vm, near, acc, cols, near_sem,
):
    peers = recv_ref.shape[0]
    blocks = s_ref.shape[1] // BLOCK
    spans = -(-rows // LANES)
    facts = recv_ref[:, CAP * rows : CAP * rows + FACTS]
    facts32[...] = facts.astype(F32).reshape(facts32.shape)

    def fact(row):
        return facts32[pl.ds(row, peers, stride=FACTS), :]

    lane = iota((peers, LANES), 1)
    routes = fact(ROUTE)
    slots = jnp.zeros((peers, LANES), F32)
    for r in range(CAP):
        mine = jnp.where(lane == me_ref[0] * CAP + r, routes, 0.0)
        slots = jnp.where(lane == r, jnp.sum(mine, axis=1, keepdims=True), slots)
    near_vm[...] = slots.astype(jnp.int32)
    near_copy = pltpu.make_async_copy(near_vm, near, near_sem)
    near_copy.start()
    for q in range(spans):
        if (q + 1) * LANES <= rows:
            values = [fact(q * VALUES + v) for v in range(VALUES)]
        else:
            values = [fact(q * VALUES + v) for v in range(VALUES // 2)]
            values += [pltpu.roll(value, LANES // 2, 1) for value in values]
        highest, high, low, s_highest, s_high, s_low = values
        raised = jnp.exp(highest - jnp.max(highest, axis=0, keepdims=True))
        total = jnp.sum(raised * (high + low), axis=0, keepdims=True)
        part = raised * ((1.0 - SMOOTH) / total)
        s_top = jnp.max(s_highest, axis=0, keepdims=True)
        s_total = jnp.sum(jnp.exp(s_highest - s_top) * (s_high + s_low), axis=0, keepdims=True)
        norm = jnp.broadcast_to(s_top + jnp.log(s_total), (LANES - peers, LANES))
        share[q * LANES : (q + 1) * LANES] = jnp.concatenate([part, norm], axis=0).T
    cols[...] = jnp.zeros(cols.shape, F32)
    near_copy.wait()

    def work(q, carry):
        at = pl.ds(pl.multiple_of(q * chunk, chunk), chunk)
        shares = share[at]
        acc[...] = jnp.zeros(acc.shape, F32)
        for source in range(peers):
            scale = jnp.broadcast_to(shares[:, source : source + 1], (chunk, LANES))
            for r in range(CAP):
                piece = recv_ref[source, pl.ds(pl.multiple_of(r * rows + q * chunk, 16), chunk)]
                acc[near[source, r]] += scale * piece.astype(F32)
        norm = jnp.broadcast_to(shares[:, peers : peers + 1], (chunk, LANES))

        def block(j, cross):
            target = acc[j] + SMOOTH / VS
            student = s_ref[at, pl.ds(pl.multiple_of(j * BLOCK, BLOCK), BLOCK)].astype(F32)
            return cross + target * (jnp.log(target) - (student - norm))

        cross = lax.fori_loop(0, blocks, block, jnp.zeros((chunk, LANES), F32))
        cols[at] = jnp.broadcast_to(jnp.sum(cross, axis=1, keepdims=True), (chunk, LANES))
        return carry

    lax.fori_loop(0, rows // chunk, work, 0)
    counted = jnp.sum(mask_ref[...].reshape(1, -1).astype(F32), axis=1, keepdims=True)
    row = iota((8, LANES), 0)
    place = iota((8, LANES), 1)
    values = jnp.zeros((8, LANES), F32)
    part = jnp.zeros((8, LANES), F32)
    for q in range(spans):
        kl = cols[q * LANES : (q + 1) * LANES].T[:8]
        ahead = place + q * LANES
        kl = jnp.where((ahead < rows) & ((ahead + first).astype(F32) < counted), kl, 0.0)
        values = jnp.where(row % 4 == q, kl, values)
        part = part + kl
    whole_sum = jnp.broadcast_to(jnp.sum(part, axis=1, keepdims=True), (8, LANES))
    tally = jnp.where(place == 0, whole_sum, jnp.where(place == 1, counted, 0.0))
    values = jnp.where(row % 4 == 3, tally, values)
    for d in range(peers // 2):
        out_ref[d * 8 : (d + 1) * 8] = values


def tally_kernel(all_ref, out_ref):
    peers = all_ref.shape[0] // 4
    sums = jnp.sum(all_ref[pl.ds(3, peers, stride=4), :], axis=0, keepdims=True)
    lane = iota((1, LANES), 1)
    sums = jnp.where(lane == 1, sums * (1.0 / peers), sums)
    out_ref[...] = jnp.broadcast_to(sums, out_ref.shape)


def loss_kernel(rows, first, all_ref, mask_ref, loss_ref):
    peers = all_ref.shape[0] // 4
    spans = -(-rows // LANES)
    kl = jnp.concatenate(
        [
            jnp.sum(all_ref[pl.ds(q, peers, stride=4), :], axis=0, keepdims=True)
            for q in range(spans)
        ],
        axis=1,
    )
    mask = mask_ref[...].reshape(1, -1)
    width = spans * LANES
    row = iota((16, width), 0)
    parts = jnp.zeros((16, width), F32)
    for v, part in enumerate(parted(kl, 3)):
        parts = jnp.where(row == v, jnp.broadcast_to(part, (16, width)), parts)
    back = jnp.dot(parts.astype(BF16), selector(mask, width, first), preferred_element_type=F32)
    loss = jnp.sum(back, axis=0, keepdims=True) * mask.astype(F32)
    loss_ref[...] = loss.reshape(loss_ref.shape)


def close_kernel(rows, tally_ref, mean_ref, over_ref):
    lane = iota((1, LANES), 1)
    sums = jnp.sum(tally_ref[...], axis=0, keepdims=True)
    most = jnp.max(tally_ref[...], axis=0, keepdims=True)
    total = jnp.sum(jnp.where(lane == 0, sums, 0.0), axis=1, keepdims=True)
    count = jnp.sum(jnp.where(lane == 1, sums, 0.0), axis=1, keepdims=True)
    mean_ref[0] = jnp.sum(total / count)
    over_ref[0] = jnp.max(jnp.where((lane == 1) & (most > rows), 1, 0))


def whole(memory_space):
    return pl.BlockSpec(memory_space=memory_space)


VM, SM, HB = pltpu.VMEM, pltpu.SMEM, pltpu.HBM
SMALL = pltpu.CompilerParams(vmem_limit_bytes=6 << 20)


def exchanged(teacher_logits, student_logits, dest, tile_weight, mask, rows, first):
    peers = lax.axis_size("vocab")
    groups = lax.axis_size("dp")
    me = lax.axis_index("vocab").astype(jnp.int32).reshape(1)
    tokens = teacher_logits.shape[0]
    tb_dev = teacher_logits.shape[1] // BLOCK
    sb_dev = student_logits.shape[1] // BLOCK
    wide = -(-rows // LANES) * LANES
    dma = pltpu.SemaphoreType.DMA
    tall = max(rows, LANES)
    send, kept = pl.pallas_call(
        functools.partial(send_kernel, rows, first, sb_dev),
        out_shape=(
            jax.ShapeDtypeStruct((peers, CAP * rows + FACTS, LANES), BF16),
            jax.ShapeDtypeStruct((rows, student_logits.shape[1]), BF16),
        ),
        in_specs=[whole(SM), whole(VM), whole(HB), whole(HB), whole(HB), whole(HB)],
        out_specs=(whole(VM), whole(VM)),
        scratch_shapes=[
            VM(teacher_logits.shape, BF16),
            VM(tile_weight.shape, BF16),
            VM(student_logits.shape, BF16),
            SM(dest.shape, jnp.int32),
            VM((rows, tokens), BF16),
            VM((rows, tb_dev * BLOCK), BF16),
            VM((tb_dev, BLOCK, K * BLOCK), BF16),
            VM((wide, LANES), F32),
            VM((rows, LANES), F32),
            VM((rows, LANES), F32),
            VM((rows, LANES), F32),
            VM((rows, LANES), F32),
            SM((peers,), jnp.int32),
            dma((2,)),
            dma((3,)),
            dma((1,)),
        ],
        compiler_params=pltpu.CompilerParams(vmem_limit_bytes=34 << 20),
        name="send",
    )(me, mask, dest, teacher_logits, tile_weight, student_logits)
    received = lax.all_to_all(send, "vocab", 0, 0, tiled=True)
    chunk = rows // 2 if rows % 64 == 0 else rows
    mine = pl.pallas_call(
        functools.partial(combine_kernel, rows, first, chunk),
        out_shape=jax.ShapeDtypeStruct((peers * 4, LANES), F32),
        in_specs=[whole(SM), whole(VM), whole(VM), whole(VM)],
        out_specs=whole(VM),
        scratch_shapes=[
            VM((peers * FACTS, LANES), F32),
            VM((wide, LANES), F32),
            VM((peers, LANES), jnp.int32),
            SM((peers, LANES), jnp.int32),
            VM((sb_dev + 1, chunk, LANES), F32),
            VM((wide, LANES), F32),
            dma(()),
        ],
        compiler_params=pltpu.CompilerParams(vmem_limit_bytes=20 << 20),
        name="combine",
    )(me, mask, received, kept)
    collected = lax.all_to_all(mine, "vocab", 0, 0, tiled=True)
    tally = pl.pallas_call(
        tally_kernel,
        out_shape=jax.ShapeDtypeStruct((groups, LANES), F32),
        in_specs=[whole(VM)],
        out_specs=whole(VM),
        compiler_params=SMALL,
        name="tally",
    )(collected)
    tally = lax.all_to_all(tally, "dp", 0, 0, tiled=True)
    loss = pl.pallas_call(
        functools.partial(loss_kernel, rows, first),
        out_shape=jax.ShapeDtypeStruct((tokens,), F32),
        in_specs=[whole(VM), whole(VM)],
        out_specs=whole(VM),
        cost_estimate=pl.CostEstimate(flops=10**10, bytes_accessed=10**6, transcendentals=0),
        compiler_params=SMALL,
        name="loss",
    )(collected, mask)
    mean, over = pl.pallas_call(
        functools.partial(close_kernel, rows),
        out_shape=(jax.ShapeDtypeStruct((1,), F32), jax.ShapeDtypeStruct((1,), jnp.int32)),
        in_specs=[whole(VM)],
        out_specs=(whole(SM), whole(SM)),
        compiler_params=SMALL,
        name="close",
    )(tally)
    return loss, mean.reshape(()), over.reshape(())


def local(teacher_logits, student_logits, tile_dest, tile_weight, token_mask):
    tokens = teacher_logits.shape[0]
    parts = (teacher_logits, student_logits, tile_dest.T, tile_weight, token_mask)
    rows = tokens * 5 // 6 if tokens % 384 == 0 else tokens
    loss, mean, over = exchanged(*parts, rows, 0)
    if rows < tokens:

        def rest():
            more, more_mean, _ = exchanged(*parts, tokens - rows, rows)
            return loss + more, mean + more_mean

        loss, mean = lax.cond(over > 0, rest, lambda: (loss, mean))
    return loss, mean


def solution(mesh):
    in_specs = (P("dp", "vocab"), P("dp", "vocab"), P(), P("vocab", None, None, None), P("dp"))
    out_specs = (P("dp"), P())
    return jax.shard_map(local, mesh=mesh, in_specs=in_specs, out_specs=out_specs, check_vma=False)
```

```python
import functools

import jax
import jax.numpy as jnp
from jax import lax
from jax.experimental import pallas as pl
from jax.experimental.pallas import tpu as pltpu
from jax.sharding import PartitionSpec as P

BLOCK = 128
VS = 126976
K = 2
CAP = 3
SMOOTH = 0.1
LANES = 128
GROUP = 8
VALUES = 6
F32 = jnp.float32
BF16 = jnp.bfloat16


def fact_rows(rows):
    full, rest = divmod(rows, LANES)
    needed = VALUES * full + (rest > 0) * VALUES // (1 + (rest <= LANES // 2)) + 1
    return -(-needed // 16) * 16


def iota(shape, dim):
    return lax.broadcasted_iota(jnp.int32, shape, dim)


def selector(mask_row, rows, first):
    tokens = mask_row.shape[1]
    before = (iota((tokens, tokens), 0) < iota((tokens, tokens), 1)).astype(F32).astype(BF16)
    kept = jnp.broadcast_to(mask_row.astype(F32), (16, tokens)).astype(BF16)
    rank = jnp.dot(kept, before, preferred_element_type=F32)[0:1]
    wanted = (iota((rows, tokens), 0) + first).astype(F32)
    hit = (wanted == jnp.broadcast_to(rank, (rows, tokens))) & (
        jnp.broadcast_to(mask_row, (rows, tokens)) > 0
    )
    return hit.astype(F32).astype(BF16)


def parted(value, count):
    out = []
    for _ in range(count):
        out.append(value.astype(BF16).astype(F32))
        value = value - out[-1]
    return out


def in_lanes(columns, rows):
    lane = iota((rows, LANES), 1)
    out = jnp.zeros((rows, LANES), F32)
    for v, column in enumerate(columns):
        out = jnp.where(lane == v, jnp.broadcast_to(column, (rows, LANES)), out)
    return out


def column_copies(hbm, buf, sems, blocks, parts):
    groups = blocks // GROUP
    cuts = [groups * i // parts for i in range(parts + 1)]
    out = []
    for c, (lo, hi) in enumerate(zip(cuts[:-1], cuts[1:])):
        end = hi * GROUP if c < parts - 1 else blocks
        where = (slice(None), pl.ds(lo * GROUP * BLOCK, (end - lo * GROUP) * BLOCK))
        copy = pltpu.make_async_copy(hbm.at[where], buf.at[where], sems.at[c])
        copy.start()
        out.append(((lo, hi), copy))
    return out


def picked(sel_ref, src_ref, dst_ref, top_ref, start, count):
    tops = []
    for i in range(0, count, 2):
        width = min(2, count - i) * BLOCK
        at = pl.ds(start + i * BLOCK, width)
        got = jnp.dot(sel_ref[...], src_ref[:, at], preferred_element_type=F32)
        dst_ref[:, at] = got.astype(BF16)
        tops += [got[:, j : j + BLOCK] for j in range(0, width, BLOCK)]
    top_ref[...] = functools.reduce(jnp.maximum, tops, top_ref[...])


def size_kernel(sizes, mask_ref, which_ref):
    kept = jnp.sum(mask_ref[...].reshape(1, -1).astype(F32))
    which_ref[0] = sum((kept > size).astype(jnp.int32) for size in sizes[:-1]) + 0


def send_kernel(
    rows, first, sb_dev,
    me_ref, mask_ref, dest_hbm, x_hbm, w_hbm, s_hbm, send_ref, kept,
    x_buf, w_buf, s_buf, dest, sel, xc, maps, cols,
    top, total, s_top, s_total, used,
    in_sem, x_sem, s_sem,
):
    blocks = w_buf.shape[0]
    s_blocks = s_buf.shape[1] // BLOCK
    peers = send_ref.shape[0]
    w_copy = pltpu.make_async_copy(w_hbm, w_buf, in_sem.at[0])
    w_copy.start()
    x_copies = column_copies(x_hbm, x_buf, x_sem, blocks, 3)
    ((_, s_copy),) = column_copies(s_hbm, s_buf, s_sem, s_blocks, 1)
    dest_copy = pltpu.make_async_copy(dest_hbm, dest, in_sem.at[1])
    dest_copy.start()
    sel[...] = selector(mask_ref[...].reshape(1, -1), rows, first)
    top[...] = jnp.full(top.shape, -jnp.inf, F32)
    s_top[...] = jnp.full(top.shape, -jnp.inf, F32)
    total[...] = jnp.zeros(total.shape, F32)
    s_total[...] = jnp.zeros(total.shape, F32)

    def clear(i, carry):
        used[i] = 0
        return carry

    lax.fori_loop(0, peers, clear, 0)
    w_copy.wait()
    ones = jnp.ones((K * BLOCK, BLOCK), BF16)

    def weight(b):
        both = jnp.concatenate([w_buf[b, k] for k in range(K)], axis=1)
        scale = 1.0 / jnp.dot(both, ones, preferred_element_type=F32)
        maps[b] = (both.astype(F32) * jnp.concatenate([scale] * K, axis=1)).astype(BF16)

    def teacher(i, count):
        start = i * GROUP * BLOCK
        if not isinstance(i, int):
            start = pl.multiple_of(start, GROUP * BLOCK)
        picked(sel, x_buf, xc, top, start, count)
        for j in range(count):
            weight(i * GROUP + j)

    def teachers(i, carry):
        teacher(i, GROUP)
        return carry

    for (lo, hi), copy in x_copies:
        copy.wait()
        lax.fori_loop(lo, hi, teachers, 0)
    if blocks % GROUP:
        teacher(blocks // GROUP, blocks % GROUP)
    highest = jnp.max(top[...], axis=1, keepdims=True)
    top[...] = jnp.broadcast_to(highest, top.shape)
    dest_copy.wait()
    s_copy.wait()
    base = me_ref[0] * blocks
    factor = (1 << 16) // sb_dev + 1
    assert all(d * factor >> 16 == d // sb_dev for d in range(peers * sb_dev))
    lane = iota((8, LANES), 1)

    def raised(b):
        at = pl.ds(pl.multiple_of(b * BLOCK, BLOCK), BLOCK)
        return jnp.exp(xc[:, at].astype(F32) - top[...])

    def tile(b, value, route):
        mapped = jnp.dot(value.astype(BF16), maps[b], preferred_element_type=F32)
        for k in range(K):
            block = dest[k, base + b]
            owner = lax.shift_right_logical(block * factor, 16)
            rank = used[owner]
            used[owner] = rank + 1
            near = (block - owner * sb_dev).astype(F32)
            route = jnp.where(lane == owner * CAP + rank, near, route)
            at = pl.ds(pl.multiple_of(rank * rows, 16), rows)
            send_ref[owner, at] = mapped[:, k * BLOCK : (k + 1) * BLOCK].astype(BF16)
        return route

    def pair(i, route):
        one, two = raised(2 * i), raised(2 * i + 1)
        total[...] += one + two
        return tile(2 * i + 1, two, tile(2 * i, one, route))

    def both(i, route):
        picked(sel, s_buf, kept, s_top, pl.multiple_of(i * 4 * BLOCK, 4 * BLOCK), 4)
        return pair(2 * i + 1, pair(2 * i, route))

    shared = min(blocks, s_blocks) // 4 * 2
    route = lax.fori_loop(0, shared // 2, both, jnp.full((8, LANES), sb_dev, F32))
    for i in range(shared, blocks // 2):
        route = pair(i, route)
    for b in range(2 * shared, s_blocks, 2):
        picked(sel, s_buf, kept, s_top, b * BLOCK, min(2, s_blocks - b))
    if blocks % 2:
        last = raised(blocks - 1)
        total[...] += last
        route = tile(blocks - 1, last, route)
    summed = jnp.sum(total[...], axis=1, keepdims=True)
    s_highest = jnp.max(s_top[...], axis=1, keepdims=True)
    s_top[...] = jnp.broadcast_to(s_highest, top.shape)

    def student(start, count):
        at = [pl.ds(start + i * BLOCK, BLOCK) for i in range(count)]
        s_total[...] += sum(jnp.exp(kept[:, a].astype(F32) - s_top[...]) for a in at)

    def students(i, carry):
        student(pl.multiple_of(i * GROUP * BLOCK, GROUP * BLOCK), GROUP)
        return carry

    lax.fori_loop(0, s_blocks // GROUP, students, 0)
    if s_blocks % GROUP:
        student(s_blocks // GROUP * GROUP * BLOCK, s_blocks % GROUP)
    s_summed = jnp.sum(s_total[...], axis=1, keepdims=True)
    columns = (highest, *parted(summed, 2), s_highest, *parted(s_summed, 2))
    full, rest = divmod(rows, LANES)
    half = 0 < rest <= LANES // 2
    facts = fact_rows(rows)
    cols[...] = jnp.zeros(cols.shape, F32)
    cols[0:rows] = in_lanes(columns, rows)
    if half:
        upper = [column[full * LANES :] for column in columns[VALUES // 2 :]]
        cols[full * LANES + LANES // 2 : full * LANES + LANES // 2 + rest] = in_lanes(upper, rest)
    total[0:facts] = jnp.zeros((facts, LANES), F32)
    for q in range(full + (rest > 0)):
        turned = cols[q * LANES : (q + 1) * LANES].T
        height = VALUES // 2 if half and q == full else VALUES
        total[q * VALUES : q * VALUES + height] = turned[:height]
    total[facts - 1 : facts] = route[0:1]
    packed = total[0:facts].astype(BF16)
    for d in range(peers):
        send_ref[d, CAP * rows : CAP * rows + facts] = packed


def combine_kernel(
    rows, first,
    me_ref, mask_ref, recv_ref, s_ref, out_ref,
    facts32, share, near_vm, near, acc, cols, near_sem,
):
    peers = recv_ref.shape[0]
    blocks = s_ref.shape[1] // BLOCK
    spans = -(-rows // LANES)
    facts = fact_rows(rows)
    arrived = recv_ref[:, CAP * rows : CAP * rows + facts]
    facts32[...] = arrived.astype(F32).reshape(facts32.shape)

    def fact(row):
        return facts32[pl.ds(row, peers, stride=facts), :]

    lane = iota((peers, LANES), 1)
    routes = fact(facts - 1)
    slots = jnp.zeros((peers, LANES), F32)
    for r in range(CAP):
        mine = jnp.where(lane == me_ref[0] * CAP + r, routes, 0.0)
        slots = jnp.where(lane == r, jnp.sum(mine, axis=1, keepdims=True), slots)
    near_vm[...] = slots.astype(jnp.int32)
    near_copy = pltpu.make_async_copy(near_vm, near, near_sem)
    near_copy.start()
    for q in range(spans):
        if rows - q * LANES > LANES // 2:
            values = [fact(q * VALUES + v) for v in range(VALUES)]
        else:
            values = [fact(q * VALUES + v) for v in range(VALUES // 2)]
            values += [pltpu.roll(value, LANES // 2, 1) for value in values]
        highest, high, low, s_highest, s_high, s_low = values
        raised = jnp.exp(highest - jnp.max(highest, axis=0, keepdims=True))
        total = jnp.sum(raised * (high + low), axis=0, keepdims=True)
        part = raised * ((1.0 - SMOOTH) / total)
        s_top = jnp.max(s_highest, axis=0, keepdims=True)
        s_total = jnp.sum(jnp.exp(s_highest - s_top) * (s_high + s_low), axis=0, keepdims=True)
        norm = jnp.broadcast_to(s_top + jnp.log(s_total), (LANES - peers, LANES))
        share[q * LANES : (q + 1) * LANES] = jnp.concatenate([part, norm], axis=0).T
    cols[...] = jnp.zeros(cols.shape, F32)
    near_copy.wait()

    def work(start, chunk):
        at = pl.ds(start, chunk)
        inner = pl.ds(0, chunk)
        shares = share[at]
        acc[:, inner] = jnp.zeros((blocks + 1, chunk, LANES), F32)

        def sources(i, turned):
            for j in range(GROUP):
                source = i * GROUP + j
                scale = jnp.broadcast_to(turned[:, j : j + 1], (chunk, LANES))
                for r in range(CAP):
                    piece = recv_ref[source, pl.ds(r * rows + start, chunk)]
                    acc[near[source, r], inner] += scale * piece.astype(F32)
            return pltpu.roll(turned, LANES - GROUP, 1)

        lax.fori_loop(0, peers // GROUP, sources, shares)
        norm = jnp.broadcast_to(shares[:, peers : peers + 1], (chunk, LANES))

        def block(j, cross):
            target = acc[j, inner] + SMOOTH / VS
            student = s_ref[at, pl.ds(pl.multiple_of(j * BLOCK, BLOCK), BLOCK)].astype(F32)
            return cross + target * (jnp.log(target) - (student - norm))

        cross = lax.fori_loop(0, blocks, block, jnp.zeros((chunk, LANES), F32))
        cols[at] = jnp.broadcast_to(jnp.sum(cross, axis=1, keepdims=True), (chunk, LANES))

    for start in range(0, rows, acc.shape[1]):
        work(start, min(acc.shape[1], rows - start))
    counted = jnp.sum(mask_ref[...].reshape(1, -1).astype(F32), axis=1, keepdims=True)
    row = iota((8, LANES), 0)
    place = iota((8, LANES), 1)
    values = jnp.zeros((8, LANES), F32)
    part = jnp.zeros((8, LANES), F32)
    for q in range(spans):
        kl = cols[q * LANES : (q + 1) * LANES].T[:8]
        ahead = place + q * LANES
        kl = jnp.where((ahead < rows) & ((ahead + first).astype(F32) < counted), kl, 0.0)
        values = jnp.where(row % 4 == q, kl, values)
        part = part + kl
    whole_sum = jnp.broadcast_to(jnp.sum(part, axis=1, keepdims=True), (8, LANES))
    tally = jnp.where(place == 0, whole_sum, jnp.where(place == 1, counted, 0.0))
    values = jnp.where(row % 4 == 3, tally, values)
    for d in range(peers // 2):
        out_ref[d * 8 : (d + 1) * 8] = values


def tally_kernel(all_ref, out_ref):
    peers = all_ref.shape[0] // 4
    sums = jnp.sum(all_ref[pl.ds(3, peers, stride=4), :], axis=0, keepdims=True)
    lane = iota((1, LANES), 1)
    sums = jnp.where(lane == 1, sums * (1.0 / peers), sums)
    out_ref[...] = jnp.broadcast_to(sums, out_ref.shape)


def loss_kernel(rows, first, all_ref, mask_ref, loss_ref):
    peers = all_ref.shape[0] // 4
    spans = -(-rows // LANES)
    kl = jnp.concatenate(
        [
            jnp.sum(all_ref[pl.ds(q, peers, stride=4), :], axis=0, keepdims=True)
            for q in range(spans)
        ],
        axis=1,
    )
    mask = mask_ref[...].reshape(1, -1)
    width = spans * LANES
    row = iota((16, width), 0)
    parts = jnp.zeros((16, width), F32)
    for v, part in enumerate(parted(kl, 3)):
        parts = jnp.where(row == v, jnp.broadcast_to(part, (16, width)), parts)
    back = jnp.dot(parts.astype(BF16), selector(mask, width, first), preferred_element_type=F32)
    loss = jnp.sum(back, axis=0, keepdims=True) * mask.astype(F32)
    loss_ref[...] = loss.reshape(loss_ref.shape)


def close_kernel(tally_ref, mean_ref):
    lane = iota((1, LANES), 1)
    sums = jnp.sum(tally_ref[...], axis=0, keepdims=True)
    total = jnp.sum(jnp.where(lane == 0, sums, 0.0), axis=1, keepdims=True)
    count = jnp.sum(jnp.where(lane == 1, sums, 0.0), axis=1, keepdims=True)
    mean_ref[0] = jnp.sum(total / count)


def whole(memory_space):
    return pl.BlockSpec(memory_space=memory_space)


VM, SM, HB = pltpu.VMEM, pltpu.SMEM, pltpu.HBM
SMALL = pltpu.CompilerParams(vmem_limit_bytes=6 << 20)


def exchanged(rows, first, teacher_logits, student_logits, dest, tile_weight, mask):
    peers = lax.axis_size("vocab")
    groups = lax.axis_size("dp")
    me = lax.axis_index("vocab").astype(jnp.int32).reshape(1)
    tokens = teacher_logits.shape[0]
    tb_dev = teacher_logits.shape[1] // BLOCK
    sb_dev = student_logits.shape[1] // BLOCK
    wide = -(-rows // LANES) * LANES
    facts = fact_rows(rows)
    dma = pltpu.SemaphoreType.DMA
    tall = max(rows, LANES)
    send, kept = pl.pallas_call(
        functools.partial(send_kernel, rows, first, sb_dev),
        out_shape=(
            jax.ShapeDtypeStruct((peers, CAP * rows + facts, LANES), BF16),
            jax.ShapeDtypeStruct((rows, student_logits.shape[1]), BF16),
        ),
        in_specs=[whole(SM), whole(VM), whole(HB), whole(HB), whole(HB), whole(HB)],
        out_specs=(whole(VM), whole(VM)),
        scratch_shapes=[
            VM(teacher_logits.shape, BF16),
            VM(tile_weight.shape, BF16),
            VM(student_logits.shape, BF16),
            SM(dest.shape, jnp.int32),
            VM((rows, tokens), BF16),
            VM((rows, tb_dev * BLOCK), BF16),
            VM((tb_dev, BLOCK, K * BLOCK), BF16),
            VM((wide, LANES), F32),
            VM((rows, LANES), F32),
            VM((rows, LANES), F32),
            VM((rows, LANES), F32),
            VM((rows, LANES), F32),
            SM((peers,), jnp.int32),
            dma((2,)),
            dma((3,)),
            dma((1,)),
        ],
        compiler_params=pltpu.CompilerParams(vmem_limit_bytes=34 << 20),
        name="send",
    )(me, mask, dest, teacher_logits, tile_weight, student_logits)
    received = lax.all_to_all(send, "vocab", 0, 0, tiled=True)
    chunk = -(-rows // 32) * 16
    mine = pl.pallas_call(
        functools.partial(combine_kernel, rows, first),
        out_shape=jax.ShapeDtypeStruct((peers * 4, LANES), F32),
        in_specs=[whole(SM), whole(VM), whole(VM), whole(VM)],
        out_specs=whole(VM),
        scratch_shapes=[
            VM((peers * facts, LANES), F32),
            VM((wide, LANES), F32),
            VM((peers, LANES), jnp.int32),
            SM((peers, LANES), jnp.int32),
            VM((sb_dev + 1, chunk, LANES), F32),
            VM((wide, LANES), F32),
            dma(()),
        ],
        compiler_params=pltpu.CompilerParams(vmem_limit_bytes=20 << 20),
        name="combine",
    )(me, mask, received, kept)
    collected = lax.all_to_all(mine, "vocab", 0, 0, tiled=True)
    tally = pl.pallas_call(
        tally_kernel,
        out_shape=jax.ShapeDtypeStruct((groups, LANES), F32),
        in_specs=[whole(VM)],
        out_specs=whole(VM),
        compiler_params=SMALL,
        name="tally",
    )(collected)
    loss = pl.pallas_call(
        functools.partial(loss_kernel, rows, first),
        out_shape=jax.ShapeDtypeStruct((tokens,), F32),
        in_specs=[whole(VM), whole(VM)],
        out_specs=whole(VM),
        cost_estimate=pl.CostEstimate(flops=10**10, bytes_accessed=10**6, transcendentals=0),
        compiler_params=SMALL,
        name="loss",
    )(collected, mask)
    return loss, tally


def local(teacher_logits, student_logits, tile_dest, tile_weight, token_mask):
    tokens = teacher_logits.shape[0]
    parts = (teacher_logits, student_logits, tile_dest.T, tile_weight, token_mask)
    sizes = [tokens]
    if tokens % 384 == 0:
        sizes = [tokens // 384 * size for size in (304, 320, 384)]
    which = pl.pallas_call(
        functools.partial(size_kernel, sizes),
        out_shape=jax.ShapeDtypeStruct((1,), jnp.int32),
        in_specs=[whole(VM)],
        out_specs=whole(SM),
        compiler_params=SMALL,
        name="size",
    )(token_mask)
    loss, tally = lax.switch(which.reshape(()), [functools.partial(exchanged, size, 0) for size in sizes], *parts)
    tally = lax.all_to_all(tally, "dp", 0, 0, tiled=True)
    mean = pl.pallas_call(
        close_kernel,
        out_shape=jax.ShapeDtypeStruct((1,), F32),
        in_specs=[whole(VM)],
        out_specs=whole(SM),
        compiler_params=SMALL,
        name="close",
    )(tally)
    return loss, mean.reshape(())


def solution(mesh):
    in_specs = (P("dp", "vocab"), P("dp", "vocab"), P(), P("vocab", None, None, None), P("dp"))
    out_specs = (P("dp"), P())
    return jax.shard_map(local, mesh=mesh, in_specs=in_specs, out_specs=out_specs, check_vma=False)
```

```python
import functools

import jax
import jax.numpy as jnp
from jax import lax
from jax.experimental import pallas as pl
from jax.experimental.pallas import tpu as pltpu
from jax.sharding import PartitionSpec as P

BLOCK = 128
VS = 126976
K = 2
CAP = 3
SMOOTH = 0.1
LANES = 128
GROUP = 12
SOURCES = 32
VALUES = 6
F32 = jnp.float32
BF16 = jnp.bfloat16


def fact_rows(rows):
    full, rest = divmod(rows, LANES)
    needed = VALUES * full + (rest > 0) * VALUES // (1 + (rest <= LANES // 2)) + 1
    return -(-needed // 16) * 16


def iota(shape, dim):
    return lax.broadcasted_iota(jnp.int32, shape, dim)


def selector(mask_row, rows, first):
    tokens = mask_row.shape[1]
    before = (iota((tokens, tokens), 0) < iota((tokens, tokens), 1)).astype(F32).astype(BF16)
    kept = jnp.broadcast_to(mask_row.astype(F32), (16, tokens)).astype(BF16)
    rank = jnp.dot(kept, before, preferred_element_type=F32)[0:1]
    wanted = (iota((rows, tokens), 0) + first).astype(F32)
    hit = (wanted == jnp.broadcast_to(rank, (rows, tokens))) & (
        jnp.broadcast_to(mask_row, (rows, tokens)) > 0
    )
    return hit.astype(F32).astype(BF16)


def parted(value, count):
    out = []
    for _ in range(count):
        out.append(value.astype(BF16).astype(F32))
        value = value - out[-1]
    return out


def in_lanes(columns, rows):
    lane = iota((rows, LANES), 1)
    out = jnp.zeros((rows, LANES), F32)
    for v, column in enumerate(columns):
        out = jnp.where(lane == v, jnp.broadcast_to(column, (rows, LANES)), out)
    return out


def column_copies(hbm, buf, sems, blocks, parts, beside=None):
    groups = blocks // GROUP
    cuts = [groups * i // parts for i in range(parts + 1)]
    out = []
    for c, (lo, hi) in enumerate(zip(cuts[:-1], cuts[1:])):
        end = hi * GROUP if c < parts - 1 else blocks
        copies = []
        if beside:
            run = pl.ds(lo * GROUP, end - lo * GROUP)
            copies.append(
                pltpu.make_async_copy(beside[0].at[run], beside[1].at[run], beside[2].at[c])
            )
        where = (slice(None), pl.ds(lo * GROUP * BLOCK, (end - lo * GROUP) * BLOCK))
        copies.append(pltpu.make_async_copy(hbm.at[where], buf.at[where], sems.at[c]))
        for copy in copies:
            copy.start()
        out.append(((lo, hi), *copies))
    return out


def picked(sel_ref, src_ref, dst_ref, top_ref, start, count):
    tops = []
    for i in range(0, count, 2):
        width = min(2, count - i) * BLOCK
        at = pl.ds(start + i * BLOCK, width)
        got = jnp.dot(sel_ref[...], src_ref[:, at], preferred_element_type=F32)
        dst_ref[:, at] = got.astype(BF16)
        tops += [got[:, j : j + BLOCK] for j in range(0, width, BLOCK)]
    top_ref[...] = functools.reduce(jnp.maximum, tops, top_ref[...])


def size_kernel(sizes, mask_ref, which_ref):
    kept = jnp.sum(mask_ref[...].reshape(1, -1).astype(F32))
    which_ref[0] = sum((kept > size).astype(jnp.int32) for size in sizes[:-1]) + 0


def send_kernel(
    rows, first, sb_dev,
    me_ref, mask_ref, dest_hbm, x_hbm, w_hbm, s_hbm, send_ref, kept,
    x_buf, w_buf, s_buf, dest, sel, xc, maps, cols,
    top, total, s_top, s_total, used,
    in_sem, w_sem, x_sem, s_sem,
):
    blocks = w_buf.shape[0]
    s_blocks = s_buf.shape[1] // BLOCK
    peers = send_ref.shape[0]
    x_copies = column_copies(x_hbm, x_buf, x_sem, blocks, 3, (w_hbm, w_buf, w_sem))
    ((_, s_copy),) = column_copies(s_hbm, s_buf, s_sem, s_blocks, 1)
    dest_copy = pltpu.make_async_copy(dest_hbm, dest, in_sem)
    dest_copy.start()
    sel[...] = selector(mask_ref[...].reshape(1, -1), rows, first)
    top[...] = jnp.full(top.shape, -jnp.inf, F32)
    s_top[...] = jnp.full(top.shape, -jnp.inf, F32)
    total[...] = jnp.zeros(total.shape, F32)
    s_total[...] = jnp.zeros(total.shape, F32)

    def clear(i, carry):
        used[i] = 0
        return carry

    lax.fori_loop(0, peers, clear, 0)
    ones = jnp.ones((K * BLOCK, BLOCK), BF16)

    def weight(b):
        both = jnp.concatenate([w_buf[b, k] for k in range(K)], axis=1)
        scale = 1.0 / jnp.dot(both, ones, preferred_element_type=F32)
        maps[b] = (both.astype(F32) * jnp.concatenate([scale] * K, axis=1)).astype(BF16)

    def teacher(i, count):
        start = i * GROUP * BLOCK
        if not isinstance(i, int):
            start = pl.multiple_of(start, GROUP * BLOCK)
        picked(sel, x_buf, xc, top, start, count)
        for j in range(count):
            weight(i * GROUP + j)

    def teachers(i, carry):
        teacher(i, GROUP)
        return carry

    for (lo, hi), *copies in x_copies:
        for copy in copies:
            copy.wait()
        lax.fori_loop(lo, hi, teachers, 0)
    if blocks % GROUP:
        teacher(blocks // GROUP, blocks % GROUP)
    highest = jnp.max(top[...], axis=1, keepdims=True)
    top[...] = jnp.broadcast_to(highest, top.shape)
    dest_copy.wait()
    s_copy.wait()
    base = me_ref[0] * blocks
    factor = (1 << 16) // sb_dev + 1
    assert all(d * factor >> 16 == d // sb_dev for d in range(peers * sb_dev))
    lane = iota((8, LANES), 1)

    def raised(b):
        at = pl.ds(pl.multiple_of(b * BLOCK, BLOCK), BLOCK)
        return jnp.exp(xc[:, at].astype(F32) - top[...])

    def tile(b, value, route):
        mapped = jnp.dot(value.astype(BF16), maps[b], preferred_element_type=F32)
        for k in range(K):
            block = dest[k, base + b]
            owner = lax.shift_right_logical(block * factor, 16)
            rank = used[owner]
            used[owner] = rank + 1
            near = (block - owner * sb_dev).astype(F32)
            route = jnp.where(lane == owner * CAP + rank, near, route)
            at = pl.ds(pl.multiple_of(rank * rows, 16), rows)
            send_ref[owner, at] = mapped[:, k * BLOCK : (k + 1) * BLOCK].astype(BF16)
        return route

    def pair(i, route):
        one, two = raised(2 * i), raised(2 * i + 1)
        total[...] += one + two
        return tile(2 * i + 1, two, tile(2 * i, one, route))

    def both(i, route):
        picked(sel, s_buf, kept, s_top, pl.multiple_of(i * 4 * BLOCK, 4 * BLOCK), 4)
        return pair(2 * i + 1, pair(2 * i, route))

    shared = min(blocks, s_blocks) // 4 * 2
    route = lax.fori_loop(0, shared // 2, both, jnp.full((8, LANES), sb_dev, F32))
    for i in range(shared, blocks // 2):
        route = pair(i, route)
    for b in range(2 * shared, s_blocks, 2):
        picked(sel, s_buf, kept, s_top, b * BLOCK, min(2, s_blocks - b))
    if blocks % 2:
        last = raised(blocks - 1)
        total[...] += last
        route = tile(blocks - 1, last, route)
    summed = jnp.sum(total[...], axis=1, keepdims=True)
    s_highest = jnp.max(s_top[...], axis=1, keepdims=True)
    s_top[...] = jnp.broadcast_to(s_highest, top.shape)

    def student(start, count):
        at = [pl.ds(start + i * BLOCK, BLOCK) for i in range(count)]
        s_total[...] += sum(jnp.exp(kept[:, a].astype(F32) - s_top[...]) for a in at)

    def students(i, carry):
        student(pl.multiple_of(i * GROUP * BLOCK, GROUP * BLOCK), GROUP)
        return carry

    lax.fori_loop(0, s_blocks // GROUP, students, 0)
    if s_blocks % GROUP:
        student(s_blocks // GROUP * GROUP * BLOCK, s_blocks % GROUP)
    s_summed = jnp.sum(s_total[...], axis=1, keepdims=True)
    columns = (highest, *parted(summed, 2), s_highest, *parted(s_summed, 2))
    full, rest = divmod(rows, LANES)
    half = 0 < rest <= LANES // 2
    facts = fact_rows(rows)
    cols[...] = jnp.zeros(cols.shape, F32)
    cols[0:rows] = in_lanes(columns, rows)
    if half:
        upper = [column[full * LANES :] for column in columns[VALUES // 2 :]]
        cols[full * LANES + LANES // 2 : full * LANES + LANES // 2 + rest] = in_lanes(upper, rest)
    total[0:facts] = jnp.zeros((facts, LANES), F32)
    for q in range(full + (rest > 0)):
        turned = cols[q * LANES : (q + 1) * LANES].T
        height = VALUES // 2 if half and q == full else VALUES
        total[q * VALUES : q * VALUES + height] = turned[:height]
    total[facts - 1 : facts] = route[0:1]
    packed = total[0:facts].astype(BF16)
    for d in range(peers):
        send_ref[d, CAP * rows : CAP * rows + facts] = packed


def combine_kernel(
    rows, first,
    me_ref, mask_ref, recv_ref, s_ref, out_ref,
    facts32, share, near_vm, near, acc, cols, near_sem,
):
    peers = recv_ref.shape[0]
    blocks = s_ref.shape[1] // BLOCK
    spans = -(-rows // LANES)
    facts = fact_rows(rows)
    arrived = recv_ref[:, CAP * rows : CAP * rows + facts]
    facts32[...] = arrived.astype(F32).reshape(facts32.shape)

    def fact(row):
        return facts32[pl.ds(row, peers, stride=facts), :]

    lane = iota((peers, LANES), 1)
    routes = fact(facts - 1)
    slots = jnp.zeros((peers, LANES), F32)
    for r in range(CAP):
        mine = jnp.where(lane == me_ref[0] * CAP + r, routes, 0.0)
        slots = jnp.where(lane == r, jnp.sum(mine, axis=1, keepdims=True), slots)
    near_vm[...] = slots.astype(jnp.int32)
    near_copy = pltpu.make_async_copy(near_vm, near, near_sem)
    near_copy.start()
    for q in range(spans):
        if rows - q * LANES > LANES // 2:
            values = [fact(q * VALUES + v) for v in range(VALUES)]
        else:
            values = [fact(q * VALUES + v) for v in range(VALUES // 2)]
            values += [pltpu.roll(value, LANES // 2, 1) for value in values]
        highest, high, low, s_highest, s_high, s_low = values
        raised = jnp.exp(highest - jnp.max(highest, axis=0, keepdims=True))
        total = jnp.sum(raised * (high + low), axis=0, keepdims=True)
        part = raised * ((1.0 - SMOOTH) / total)
        s_top = jnp.max(s_highest, axis=0, keepdims=True)
        s_total = jnp.sum(jnp.exp(s_highest - s_top) * (s_high + s_low), axis=0, keepdims=True)
        norm = jnp.broadcast_to(s_top + jnp.log(s_total), (LANES - peers, LANES))
        share[q * LANES : (q + 1) * LANES] = jnp.concatenate([part, norm], axis=0).T
    cols[...] = jnp.zeros(cols.shape, F32)
    near_copy.wait()

    def work(start, chunk):
        at = pl.ds(start, chunk)
        inner = pl.ds(0, chunk)
        shares = share[at]
        acc[:, inner] = jnp.zeros((blocks + 1, chunk, LANES), F32)

        def sources(i, turned):
            for j in range(SOURCES):
                source = i * SOURCES + j
                scale = jnp.broadcast_to(turned[:, j : j + 1], (chunk, LANES))
                for r in range(CAP):
                    piece = recv_ref[source, pl.ds(r * rows + start, chunk)]
                    acc[near[source, r], inner] += scale * piece.astype(F32)
            return pltpu.roll(turned, LANES - SOURCES, 1)

        lax.fori_loop(0, peers // SOURCES, sources, shares)
        norm = jnp.broadcast_to(shares[:, peers : peers + 1], (chunk, LANES))

        def block(j, cross):
            target = acc[j, inner] + SMOOTH / VS
            start_of = j * BLOCK if isinstance(j, int) else pl.multiple_of(j * BLOCK, BLOCK)
            student = s_ref[at, pl.ds(start_of, BLOCK)].astype(F32)
            return cross + target * (jnp.log(target) - (student - norm))

        def two(i, cross):
            return block(2 * i + 1, block(2 * i, cross))

        cross = lax.fori_loop(0, blocks // 2, two, jnp.zeros((chunk, LANES), F32))
        if blocks % 2:
            cross = block(blocks - 1, cross)
        cols[at] = jnp.broadcast_to(jnp.sum(cross, axis=1, keepdims=True), (chunk, LANES))

    for start in range(0, rows, acc.shape[1]):
        work(start, min(acc.shape[1], rows - start))
    counted = jnp.sum(mask_ref[...].reshape(1, -1).astype(F32), axis=1, keepdims=True)
    row = iota((8, LANES), 0)
    place = iota((8, LANES), 1)
    values = jnp.zeros((8, LANES), F32)
    part = jnp.zeros((8, LANES), F32)
    for q in range(spans):
        kl = cols[q * LANES : (q + 1) * LANES].T[:8]
        ahead = place + q * LANES
        kl = jnp.where((ahead < rows) & ((ahead + first).astype(F32) < counted), kl, 0.0)
        values = jnp.where(row % 4 == q, kl, values)
        part = part + kl
    whole_sum = jnp.broadcast_to(jnp.sum(part, axis=1, keepdims=True), (8, LANES))
    tally = jnp.where(place == 0, whole_sum, jnp.where(place == 1, counted, 0.0))
    values = jnp.where(row % 4 == 3, tally, values)
    for d in range(peers // 2):
        out_ref[d * 8 : (d + 1) * 8] = values


def tally_kernel(all_ref, out_ref):
    peers = all_ref.shape[0] // 4
    sums = jnp.sum(all_ref[pl.ds(3, peers, stride=4), :], axis=0, keepdims=True)
    lane = iota((1, LANES), 1)
    sums = jnp.where(lane == 1, sums * (1.0 / peers), sums)
    out_ref[...] = jnp.broadcast_to(sums, out_ref.shape)


def loss_kernel(rows, first, all_ref, mask_ref, loss_ref):
    peers = all_ref.shape[0] // 4
    spans = -(-rows // LANES)
    kl = jnp.concatenate(
        [
            jnp.sum(all_ref[pl.ds(q, peers, stride=4), :], axis=0, keepdims=True)
            for q in range(spans)
        ],
        axis=1,
    )
    mask = mask_ref[...].reshape(1, -1)
    width = spans * LANES
    row = iota((16, width), 0)
    parts = jnp.zeros((16, width), F32)
    for v, part in enumerate(parted(kl, 3)):
        parts = jnp.where(row == v, jnp.broadcast_to(part, (16, width)), parts)
    back = jnp.dot(parts.astype(BF16), selector(mask, width, first), preferred_element_type=F32)
    loss = jnp.sum(back, axis=0, keepdims=True) * mask.astype(F32)
    loss_ref[...] = loss.reshape(loss_ref.shape)


def close_kernel(tally_ref, mean_ref):
    lane = iota((1, LANES), 1)
    sums = jnp.sum(tally_ref[...], axis=0, keepdims=True)
    total = jnp.sum(jnp.where(lane == 0, sums, 0.0), axis=1, keepdims=True)
    count = jnp.sum(jnp.where(lane == 1, sums, 0.0), axis=1, keepdims=True)
    mean_ref[0] = jnp.sum(total / count)


def whole(memory_space):
    return pl.BlockSpec(memory_space=memory_space)


VM, SM, HB = pltpu.VMEM, pltpu.SMEM, pltpu.HBM
SMALL = pltpu.CompilerParams(vmem_limit_bytes=6 << 20)


def exchanged(rows, first, teacher_logits, student_logits, dest, tile_weight, mask):
    peers = lax.axis_size("vocab")
    groups = lax.axis_size("dp")
    me = lax.axis_index("vocab").astype(jnp.int32).reshape(1)
    tokens = teacher_logits.shape[0]
    tb_dev = teacher_logits.shape[1] // BLOCK
    sb_dev = student_logits.shape[1] // BLOCK
    wide = -(-rows // LANES) * LANES
    facts = fact_rows(rows)
    dma = pltpu.SemaphoreType.DMA
    tall = max(rows, LANES)
    send, kept = pl.pallas_call(
        functools.partial(send_kernel, rows, first, sb_dev),
        out_shape=(
            jax.ShapeDtypeStruct((peers, CAP * rows + facts, LANES), BF16),
            jax.ShapeDtypeStruct((rows, student_logits.shape[1]), BF16),
        ),
        in_specs=[whole(SM), whole(VM), whole(HB), whole(HB), whole(HB), whole(HB)],
        out_specs=(whole(VM), whole(VM)),
        scratch_shapes=[
            VM(teacher_logits.shape, BF16),
            VM(tile_weight.shape, BF16),
            VM(student_logits.shape, BF16),
            SM(dest.shape, jnp.int32),
            VM((rows, tokens), BF16),
            VM((rows, tb_dev * BLOCK), BF16),
            VM((tb_dev, BLOCK, K * BLOCK), BF16),
            VM((wide, LANES), F32),
            VM((rows, LANES), F32),
            VM((rows, LANES), F32),
            VM((rows, LANES), F32),
            VM((rows, LANES), F32),
            SM((peers,), jnp.int32),
            dma(()),
            dma((3,)),
            dma((3,)),
            dma((1,)),
        ],
        compiler_params=pltpu.CompilerParams(vmem_limit_bytes=34 << 20),
        name="send",
    )(me, mask, dest, teacher_logits, tile_weight, student_logits)
    received = lax.all_to_all(send, "vocab", 0, 0, tiled=True)
    chunk = -(-rows // 32) * 16
    mine = pl.pallas_call(
        functools.partial(combine_kernel, rows, first),
        out_shape=jax.ShapeDtypeStruct((peers * 4, LANES), F32),
        in_specs=[whole(SM), whole(VM), whole(VM), whole(VM)],
        out_specs=whole(VM),
        scratch_shapes=[
            VM((peers * facts, LANES), F32),
            VM((wide, LANES), F32),
            VM((peers, LANES), jnp.int32),
            SM((peers, LANES), jnp.int32),
            VM((sb_dev + 1, chunk, LANES), F32),
            VM((wide, LANES), F32),
            dma(()),
        ],
        compiler_params=pltpu.CompilerParams(vmem_limit_bytes=20 << 20),
        name="combine",
    )(me, mask, received, kept)
    collected = lax.all_to_all(mine, "vocab", 0, 0, tiled=True)
    tally = pl.pallas_call(
        tally_kernel,
        out_shape=jax.ShapeDtypeStruct((groups, LANES), F32),
        in_specs=[whole(VM)],
        out_specs=whole(VM),
        compiler_params=SMALL,
        name="tally",
    )(collected)
    loss = pl.pallas_call(
        functools.partial(loss_kernel, rows, first),
        out_shape=jax.ShapeDtypeStruct((tokens,), F32),
        in_specs=[whole(VM), whole(VM)],
        out_specs=whole(VM),
        cost_estimate=pl.CostEstimate(flops=10**10, bytes_accessed=10**6, transcendentals=0),
        compiler_params=SMALL,
        name="loss",
    )(collected, mask)
    return loss, tally


def local(teacher_logits, student_logits, tile_dest, tile_weight, token_mask):
    tokens = teacher_logits.shape[0]
    parts = (teacher_logits, student_logits, tile_dest.T, tile_weight, token_mask)
    sizes = [tokens]
    if tokens % 384 == 0:
        sizes = [tokens // 384 * size for size in (304, 320, 384)]
    which = pl.pallas_call(
        functools.partial(size_kernel, sizes),
        out_shape=jax.ShapeDtypeStruct((1,), jnp.int32),
        in_specs=[whole(VM)],
        out_specs=whole(SM),
        compiler_params=SMALL,
        name="size",
    )(token_mask)
    loss, tally = lax.switch(which.reshape(()), [functools.partial(exchanged, size, 0) for size in sizes], *parts)
    tally = lax.all_to_all(tally, "dp", 0, 0, tiled=True)
    mean = pl.pallas_call(
        close_kernel,
        out_shape=jax.ShapeDtypeStruct((1,), F32),
        in_specs=[whole(VM)],
        out_specs=whole(SM),
        compiler_params=SMALL,
        name="close",
    )(tally)
    return loss, mean.reshape(())


def solution(mesh):
    in_specs = (P("dp", "vocab"), P("dp", "vocab"), P(), P("vocab", None, None, None), P("dp"))
    out_specs = (P("dp"), P())
    return jax.shard_map(local, mesh=mesh, in_specs=in_specs, out_specs=out_specs, check_vma=False)
```

```python
import functools

import jax
import jax.numpy as jnp
from jax import lax
from jax.experimental import pallas as pl
from jax.experimental.pallas import tpu as pltpu
from jax.sharding import PartitionSpec as P

BLOCK = 128
VS = 126976
K = 2
CAP = 3
SMOOTH = 0.1
LANES = 128
GROUP = 12
SOURCES = 32
VALUES = 6
F32 = jnp.float32
BF16 = jnp.bfloat16


def fact_rows(rows):
    full, rest = divmod(rows, LANES)
    needed = VALUES * full + (rest > 0) * VALUES // (1 + (rest <= LANES // 2)) + 1
    return -(-needed // 16) * 16


def iota(shape, dim):
    return lax.broadcasted_iota(jnp.int32, shape, dim)


def selector(mask_row, rows, first):
    tokens = mask_row.shape[1]
    before = (iota((tokens, tokens), 0) < iota((tokens, tokens), 1)).astype(F32).astype(BF16)
    kept = jnp.broadcast_to(mask_row.astype(F32), (16, tokens)).astype(BF16)
    rank = jnp.dot(kept, before, preferred_element_type=F32)[0:1]
    wanted = (iota((rows, tokens), 0) + first).astype(F32)
    hit = (wanted == jnp.broadcast_to(rank, (rows, tokens))) & (
        jnp.broadcast_to(mask_row, (rows, tokens)) > 0
    )
    return hit.astype(F32).astype(BF16)


def parted(value, count):
    out = []
    for _ in range(count):
        out.append(value.astype(BF16).astype(F32))
        value = value - out[-1]
    return out


def in_lanes(columns, rows):
    lane = iota((rows, LANES), 1)
    out = jnp.zeros((rows, LANES), F32)
    for v, column in enumerate(columns):
        out = jnp.where(lane == v, jnp.broadcast_to(column, (rows, LANES)), out)
    return out


def column_copies(hbm, buf, sems, blocks, parts, beside=None):
    groups = blocks // GROUP
    cuts = [groups * i // parts for i in range(parts + 1)]
    out = []
    for c, (lo, hi) in enumerate(zip(cuts[:-1], cuts[1:])):
        end = hi * GROUP if c < parts - 1 else blocks
        copies = []
        if beside:
            run = pl.ds(lo * GROUP, end - lo * GROUP)
            copies.append(
                pltpu.make_async_copy(beside[0].at[run], beside[1].at[run], beside[2].at[c])
            )
        where = (slice(None), pl.ds(lo * GROUP * BLOCK, (end - lo * GROUP) * BLOCK))
        copies.append(pltpu.make_async_copy(hbm.at[where], buf.at[where], sems.at[c]))
        for copy in copies:
            copy.start()
        out.append(((lo, hi), *copies))
    return out


def picked(band, sel_ref, src_ref, dst_ref, top_ref, start, count):
    rows, tokens = sel_ref.shape
    runs = [(slice(0, rows), slice(0, tokens))]
    if band:
        runs = [
            (slice(r, min(r + LANES, rows)), slice(r, min(r + 2 * LANES, tokens)))
            for r in range(0, rows, LANES)
        ]
    tops = []
    for i in range(0, count, 2):
        width = min(2, count - i) * BLOCK
        at = pl.ds(start + i * BLOCK, width)
        got = jnp.concatenate(
            [
                jnp.dot(sel_ref[r, t], src_ref[t, at], preferred_element_type=F32)
                for r, t in runs
            ],
            axis=0,
        )
        dst_ref[:, at] = got.astype(BF16)
        tops += [got[:, j : j + BLOCK] for j in range(0, width, BLOCK)]
    top_ref[...] = functools.reduce(jnp.maximum, tops, top_ref[...])


def size_kernel(sizes, mask_ref, which_ref):
    kept = jnp.sum(mask_ref[...].reshape(1, -1).astype(F32))
    which = sum((kept > size).astype(jnp.int32) for size in sizes[:-1]) + 0
    if len(sizes) > 1:
        which = jnp.where(kept < mask_ref.shape[0] - LANES, len(sizes) - 1, which)
    which_ref[0] = which


def send_kernel(
    rows, first, band, sb_dev,
    me_ref, mask_ref, dest_hbm, x_hbm, w_hbm, s_hbm, send_ref, kept,
    x_buf, w_buf, s_buf, dest, sel, xc, maps, cols,
    top, total, s_top, s_total, used,
    in_sem, w_sem, x_sem, s_sem,
):
    blocks = w_buf.shape[0]
    s_blocks = s_buf.shape[1] // BLOCK
    peers = send_ref.shape[0]
    x_copies = column_copies(x_hbm, x_buf, x_sem, blocks, 3, (w_hbm, w_buf, w_sem))
    ((_, s_copy),) = column_copies(s_hbm, s_buf, s_sem, s_blocks, 1)
    dest_copy = pltpu.make_async_copy(dest_hbm, dest, in_sem)
    dest_copy.start()
    sel[...] = selector(mask_ref[...].reshape(1, -1), rows, first)
    top[...] = jnp.full(top.shape, -jnp.inf, F32)
    s_top[...] = jnp.full(top.shape, -jnp.inf, F32)
    total[...] = jnp.zeros(total.shape, F32)
    s_total[...] = jnp.zeros(total.shape, F32)

    def clear(i, carry):
        used[i] = 0
        return carry

    lax.fori_loop(0, peers, clear, 0)
    ones = jnp.ones((K * BLOCK, BLOCK), BF16)

    def weight(b):
        both = jnp.concatenate([w_buf[b, k] for k in range(K)], axis=1)
        scale = 1.0 / jnp.dot(both, ones, preferred_element_type=F32)
        maps[b] = (both.astype(F32) * jnp.concatenate([scale] * K, axis=1)).astype(BF16)

    def teacher(i, count):
        start = i * GROUP * BLOCK
        if not isinstance(i, int):
            start = pl.multiple_of(start, GROUP * BLOCK)
        picked(band, sel, x_buf, xc, top, start, count)
        for j in range(count):
            weight(i * GROUP + j)

    def teachers(i, carry):
        teacher(i, GROUP)
        return carry

    for (lo, hi), *copies in x_copies:
        for copy in copies:
            copy.wait()
        lax.fori_loop(lo, hi, teachers, 0)
    if blocks % GROUP:
        teacher(blocks // GROUP, blocks % GROUP)
    highest = jnp.max(top[...], axis=1, keepdims=True)
    top[...] = jnp.broadcast_to(highest, top.shape)
    dest_copy.wait()
    s_copy.wait()
    base = me_ref[0] * blocks
    factor = (1 << 16) // sb_dev + 1
    assert all(d * factor >> 16 == d // sb_dev for d in range(peers * sb_dev))
    lane = iota((8, LANES), 1)

    def raised(b):
        at = pl.ds(pl.multiple_of(b * BLOCK, BLOCK), BLOCK)
        return jnp.exp(xc[:, at].astype(F32) - top[...])

    def tile(b, value, route):
        mapped = jnp.dot(value.astype(BF16), maps[b], preferred_element_type=F32)
        for k in range(K):
            block = dest[k, base + b]
            owner = lax.shift_right_logical(block * factor, 16)
            rank = used[owner]
            used[owner] = rank + 1
            near = (block - owner * sb_dev).astype(F32)
            route = jnp.where(lane == owner * CAP + rank, near, route)
            at = pl.ds(pl.multiple_of(rank * rows, 16), rows)
            send_ref[owner, at] = mapped[:, k * BLOCK : (k + 1) * BLOCK].astype(BF16)
        return route

    def pair(i, route):
        one, two = raised(2 * i), raised(2 * i + 1)
        total[...] += one + two
        return tile(2 * i + 1, two, tile(2 * i, one, route))

    def both(i, route):
        picked(band, sel, s_buf, kept, s_top, pl.multiple_of(i * 4 * BLOCK, 4 * BLOCK), 4)
        return pair(2 * i + 1, pair(2 * i, route))

    shared = min(blocks, s_blocks) // 4 * 2
    route = lax.fori_loop(0, shared // 2, both, jnp.full((8, LANES), sb_dev, F32))
    for i in range(shared, blocks // 2):
        route = pair(i, route)
    for b in range(2 * shared, s_blocks, 2):
        picked(band, sel, s_buf, kept, s_top, b * BLOCK, min(2, s_blocks - b))
    if blocks % 2:
        last = raised(blocks - 1)
        total[...] += last
        route = tile(blocks - 1, last, route)
    summed = jnp.sum(total[...], axis=1, keepdims=True)
    s_highest = jnp.max(s_top[...], axis=1, keepdims=True)
    s_top[...] = jnp.broadcast_to(s_highest, top.shape)

    def student(start, count):
        at = [pl.ds(start + i * BLOCK, BLOCK) for i in range(count)]
        s_total[...] += sum(jnp.exp(kept[:, a].astype(F32) - s_top[...]) for a in at)

    def students(i, carry):
        student(pl.multiple_of(i * GROUP * BLOCK, GROUP * BLOCK), GROUP)
        return carry

    lax.fori_loop(0, s_blocks // GROUP, students, 0)
    if s_blocks % GROUP:
        student(s_blocks // GROUP * GROUP * BLOCK, s_blocks % GROUP)
    s_summed = jnp.sum(s_total[...], axis=1, keepdims=True)
    columns = (highest, *parted(summed, 2), s_highest, *parted(s_summed, 2))
    full, rest = divmod(rows, LANES)
    half = 0 < rest <= LANES // 2
    facts = fact_rows(rows)
    cols[...] = jnp.zeros(cols.shape, F32)
    cols[0:rows] = in_lanes(columns, rows)
    if half:
        upper = [column[full * LANES :] for column in columns[VALUES // 2 :]]
        cols[full * LANES + LANES // 2 : full * LANES + LANES // 2 + rest] = in_lanes(upper, rest)
    total[0:facts] = jnp.zeros((facts, LANES), F32)
    for q in range(full + (rest > 0)):
        turned = cols[q * LANES : (q + 1) * LANES].T
        height = VALUES // 2 if half and q == full else VALUES
        total[q * VALUES : q * VALUES + height] = turned[:height]
    total[facts - 1 : facts] = route[0:1]
    packed = total[0:facts].astype(BF16)
    for d in range(peers):
        send_ref[d, CAP * rows : CAP * rows + facts] = packed


def combine_kernel(
    rows, first,
    me_ref, mask_ref, recv_ref, s_ref, out_ref,
    facts32, share, near_vm, near, acc, cols, near_sem,
):
    peers = recv_ref.shape[0]
    blocks = s_ref.shape[1] // BLOCK
    spans = -(-rows // LANES)
    facts = fact_rows(rows)
    arrived = recv_ref[:, CAP * rows : CAP * rows + facts]
    facts32[...] = arrived.astype(F32).reshape(facts32.shape)

    def fact(row):
        return facts32[pl.ds(row, peers, stride=facts), :]

    lane = iota((peers, LANES), 1)
    routes = fact(facts - 1)
    slots = jnp.zeros((peers, LANES), F32)
    for r in range(CAP):
        mine = jnp.where(lane == me_ref[0] * CAP + r, routes, 0.0)
        slots = jnp.where(lane == r, jnp.sum(mine, axis=1, keepdims=True), slots)
    near_vm[...] = slots.astype(jnp.int32)
    near_copy = pltpu.make_async_copy(near_vm, near, near_sem)
    near_copy.start()
    for q in range(spans):
        if rows - q * LANES > LANES // 2:
            values = [fact(q * VALUES + v) for v in range(VALUES)]
        else:
            values = [fact(q * VALUES + v) for v in range(VALUES // 2)]
            values += [pltpu.roll(value, LANES // 2, 1) for value in values]
        highest, high, low, s_highest, s_high, s_low = values
        raised = jnp.exp(highest - jnp.max(highest, axis=0, keepdims=True))
        total = jnp.sum(raised * (high + low), axis=0, keepdims=True)
        part = raised * ((1.0 - SMOOTH) / total)
        s_top = jnp.max(s_highest, axis=0, keepdims=True)
        s_total = jnp.sum(jnp.exp(s_highest - s_top) * (s_high + s_low), axis=0, keepdims=True)
        norm = jnp.broadcast_to(s_top + jnp.log(s_total), (LANES - peers, LANES))
        share[q * LANES : (q + 1) * LANES] = jnp.concatenate([part, norm], axis=0).T
    cols[...] = jnp.zeros(cols.shape, F32)
    near_copy.wait()

    def work(start, chunk):
        at = pl.ds(start, chunk)
        inner = pl.ds(0, chunk)
        shares = share[at]
        acc[:, inner] = jnp.zeros((blocks + 1, chunk, LANES), F32)

        def sources(i, turned):
            for j in range(SOURCES):
                source = i * SOURCES + j
                scale = jnp.broadcast_to(turned[:, j : j + 1], (chunk, LANES))
                for r in range(CAP):
                    piece = recv_ref[source, pl.ds(r * rows + start, chunk)]
                    acc[near[source, r], inner] += scale * piece.astype(F32)
            return pltpu.roll(turned, LANES - SOURCES, 1)

        lax.fori_loop(0, peers // SOURCES, sources, shares)
        norm = jnp.broadcast_to(shares[:, peers : peers + 1], (chunk, LANES))

        def block(j, cross):
            target = acc[j, inner] + SMOOTH / VS
            start_of = j * BLOCK if isinstance(j, int) else pl.multiple_of(j * BLOCK, BLOCK)
            student = s_ref[at, pl.ds(start_of, BLOCK)].astype(F32)
            return cross + target * (jnp.log(target) - (student - norm))

        def two(i, cross):
            return block(2 * i + 1, block(2 * i, cross))

        cross = lax.fori_loop(0, blocks // 2, two, jnp.zeros((chunk, LANES), F32))
        if blocks % 2:
            cross = block(blocks - 1, cross)
        cols[at] = jnp.broadcast_to(jnp.sum(cross, axis=1, keepdims=True), (chunk, LANES))

    for start in range(0, rows, acc.shape[1]):
        work(start, min(acc.shape[1], rows - start))
    counted = jnp.sum(mask_ref[...].reshape(1, -1).astype(F32), axis=1, keepdims=True)
    row = iota((8, LANES), 0)
    place = iota((8, LANES), 1)
    values = jnp.zeros((8, LANES), F32)
    part = jnp.zeros((8, LANES), F32)
    for q in range(spans):
        kl = cols[q * LANES : (q + 1) * LANES].T[:8]
        ahead = place + q * LANES
        kl = jnp.where((ahead < rows) & ((ahead + first).astype(F32) < counted), kl, 0.0)
        values = jnp.where(row % 4 == q, kl, values)
        part = part + kl
    whole_sum = jnp.broadcast_to(jnp.sum(part, axis=1, keepdims=True), (8, LANES))
    tally = jnp.where(place == 0, whole_sum, jnp.where(place == 1, counted, 0.0))
    values = jnp.where(row % 4 == 3, tally, values)
    for d in range(peers // 2):
        out_ref[d * 8 : (d + 1) * 8] = values


def tally_kernel(all_ref, out_ref):
    peers = all_ref.shape[0] // 4
    sums = jnp.sum(all_ref[pl.ds(3, peers, stride=4), :], axis=0, keepdims=True)
    lane = iota((1, LANES), 1)
    sums = jnp.where(lane == 1, sums * (1.0 / peers), sums)
    out_ref[...] = jnp.broadcast_to(sums, out_ref.shape)


def loss_kernel(rows, first, all_ref, mask_ref, loss_ref):
    peers = all_ref.shape[0] // 4
    spans = -(-rows // LANES)
    kl = jnp.concatenate(
        [
            jnp.sum(all_ref[pl.ds(q, peers, stride=4), :], axis=0, keepdims=True)
            for q in range(spans)
        ],
        axis=1,
    )
    mask = mask_ref[...].reshape(1, -1)
    width = spans * LANES
    row = iota((16, width), 0)
    parts = jnp.zeros((16, width), F32)
    for v, part in enumerate(parted(kl, 3)):
        parts = jnp.where(row == v, jnp.broadcast_to(part, (16, width)), parts)
    back = jnp.dot(parts.astype(BF16), selector(mask, width, first), preferred_element_type=F32)
    loss = jnp.sum(back, axis=0, keepdims=True) * mask.astype(F32)
    loss_ref[...] = loss.reshape(loss_ref.shape)


def close_kernel(tally_ref, mean_ref):
    lane = iota((1, LANES), 1)
    sums = jnp.sum(tally_ref[...], axis=0, keepdims=True)
    total = jnp.sum(jnp.where(lane == 0, sums, 0.0), axis=1, keepdims=True)
    count = jnp.sum(jnp.where(lane == 1, sums, 0.0), axis=1, keepdims=True)
    mean_ref[0] = jnp.sum(total / count)


def whole(memory_space):
    return pl.BlockSpec(memory_space=memory_space)


VM, SM, HB = pltpu.VMEM, pltpu.SMEM, pltpu.HBM
SMALL = pltpu.CompilerParams(vmem_limit_bytes=6 << 20)


def exchanged(rows, band, teacher_logits, student_logits, dest, tile_weight, mask):
    first = 0
    peers = lax.axis_size("vocab")
    groups = lax.axis_size("dp")
    me = lax.axis_index("vocab").astype(jnp.int32).reshape(1)
    tokens = teacher_logits.shape[0]
    tb_dev = teacher_logits.shape[1] // BLOCK
    sb_dev = student_logits.shape[1] // BLOCK
    wide = -(-rows // LANES) * LANES
    facts = fact_rows(rows)
    dma = pltpu.SemaphoreType.DMA
    tall = max(rows, LANES)
    send, kept = pl.pallas_call(
        functools.partial(send_kernel, rows, first, band, sb_dev),
        out_shape=(
            jax.ShapeDtypeStruct((peers, CAP * rows + facts, LANES), BF16),
            jax.ShapeDtypeStruct((rows, student_logits.shape[1]), BF16),
        ),
        in_specs=[whole(SM), whole(VM), whole(HB), whole(HB), whole(HB), whole(HB)],
        out_specs=(whole(VM), whole(VM)),
        scratch_shapes=[
            VM(teacher_logits.shape, BF16),
            VM(tile_weight.shape, BF16),
            VM(student_logits.shape, BF16),
            SM(dest.shape, jnp.int32),
            VM((rows, tokens), BF16),
            VM((rows, tb_dev * BLOCK), BF16),
            VM((tb_dev, BLOCK, K * BLOCK), BF16),
            VM((wide, LANES), F32),
            VM((rows, LANES), F32),
            VM((rows, LANES), F32),
            VM((rows, LANES), F32),
            VM((rows, LANES), F32),
            SM((peers,), jnp.int32),
            dma(()),
            dma((3,)),
            dma((3,)),
            dma((1,)),
        ],
        compiler_params=pltpu.CompilerParams(vmem_limit_bytes=34 << 20),
        name="send",
    )(me, mask, dest, teacher_logits, tile_weight, student_logits)
    received = lax.all_to_all(send, "vocab", 0, 0, tiled=True)
    chunk = -(-rows // 32) * 16
    mine = pl.pallas_call(
        functools.partial(combine_kernel, rows, first),
        out_shape=jax.ShapeDtypeStruct((peers * 4, LANES), F32),
        in_specs=[whole(SM), whole(VM), whole(VM), whole(VM)],
        out_specs=whole(VM),
        scratch_shapes=[
            VM((peers * facts, LANES), F32),
            VM((wide, LANES), F32),
            VM((peers, LANES), jnp.int32),
            SM((peers, LANES), jnp.int32),
            VM((sb_dev + 1, chunk, LANES), F32),
            VM((wide, LANES), F32),
            dma(()),
        ],
        compiler_params=pltpu.CompilerParams(vmem_limit_bytes=20 << 20),
        name="combine",
    )(me, mask, received, kept)
    collected = lax.all_to_all(mine, "vocab", 0, 0, tiled=True)
    tally = pl.pallas_call(
        tally_kernel,
        out_shape=jax.ShapeDtypeStruct((groups, LANES), F32),
        in_specs=[whole(VM)],
        out_specs=whole(VM),
        compiler_params=SMALL,
        name="tally",
    )(collected)
    loss = pl.pallas_call(
        functools.partial(loss_kernel, rows, first),
        out_shape=jax.ShapeDtypeStruct((tokens,), F32),
        in_specs=[whole(VM), whole(VM)],
        out_specs=whole(VM),
        cost_estimate=pl.CostEstimate(flops=10**10, bytes_accessed=10**6, transcendentals=0),
        compiler_params=SMALL,
        name="loss",
    )(collected, mask)
    return loss, tally


def local(teacher_logits, student_logits, tile_dest, tile_weight, token_mask):
    tokens = teacher_logits.shape[0]
    parts = (teacher_logits, student_logits, tile_dest.T, tile_weight, token_mask)
    sizes = [tokens]
    if tokens % 384 == 0:
        sizes = [tokens // 384 * size for size in (304, 320, 384)]
    which = pl.pallas_call(
        functools.partial(size_kernel, sizes),
        out_shape=jax.ShapeDtypeStruct((1,), jnp.int32),
        in_specs=[whole(VM)],
        out_specs=whole(SM),
        compiler_params=SMALL,
        name="size",
    )(token_mask)
    loss, tally = lax.switch(which.reshape(()), [functools.partial(exchanged, size, size < tokens) for size in sizes], *parts)
    tally = lax.all_to_all(tally, "dp", 0, 0, tiled=True)
    mean = pl.pallas_call(
        close_kernel,
        out_shape=jax.ShapeDtypeStruct((1,), F32),
        in_specs=[whole(VM)],
        out_specs=whole(SM),
        compiler_params=SMALL,
        name="close",
    )(tally)
    return loss, mean.reshape(())


def solution(mesh):
    in_specs = (P("dp", "vocab"), P("dp", "vocab"), P(), P("vocab", None, None, None), P("dp"))
    out_specs = (P("dp"), P())
    return jax.shard_map(local, mesh=mesh, in_specs=in_specs, out_specs=out_specs, check_vma=False)
```

```python
import functools

import jax
import jax.numpy as jnp
from jax import lax
from jax.experimental import pallas as pl
from jax.experimental.pallas import tpu as pltpu
from jax.sharding import PartitionSpec as P

BLOCK = 128
VS = 126976
K = 2
CAP = 3
SMOOTH = 0.1
LANES = 128
GROUP = 12
SOURCES = 32
STEP = 4
VALUES = 6
F32 = jnp.float32
BF16 = jnp.bfloat16


def fact_rows(rows):
    full, rest = divmod(rows, LANES)
    needed = VALUES * full + (rest > 0) * VALUES // (1 + (rest <= LANES // 2)) + 1
    return -(-needed // 16) * 16


def iota(shape, dim):
    return lax.broadcasted_iota(jnp.int32, shape, dim)


def selector(mask_row, rows, first):
    tokens = mask_row.shape[1]
    before = (iota((tokens, tokens), 0) < iota((tokens, tokens), 1)).astype(F32).astype(BF16)
    kept = jnp.broadcast_to(mask_row.astype(F32), (16, tokens)).astype(BF16)
    rank = jnp.dot(kept, before, preferred_element_type=F32)[0:1]
    wanted = (iota((rows, tokens), 0) + first).astype(F32)
    hit = (wanted == jnp.broadcast_to(rank, (rows, tokens))) & (
        jnp.broadcast_to(mask_row, (rows, tokens)) > 0
    )
    return hit.astype(F32).astype(BF16)


def parted(value, count):
    out = []
    for _ in range(count):
        out.append(value.astype(BF16).astype(F32))
        value = value - out[-1]
    return out


def in_lanes(columns, rows):
    lane = iota((rows, LANES), 1)
    out = jnp.zeros((rows, LANES), F32)
    for v, column in enumerate(columns):
        out = jnp.where(lane == v, jnp.broadcast_to(column, (rows, LANES)), out)
    return out


def column_copies(hbm, buf, sems, blocks, parts, beside=None):
    groups = blocks // GROUP
    cuts = [groups * i // parts for i in range(parts + 1)]
    out = []
    for c, (lo, hi) in enumerate(zip(cuts[:-1], cuts[1:])):
        end = hi * GROUP if c < parts - 1 else blocks
        copies = []
        if beside:
            run = pl.ds(lo * GROUP, end - lo * GROUP)
            copies.append(
                pltpu.make_async_copy(beside[0].at[run], beside[1].at[run], beside[2].at[c])
            )
        where = (slice(None), pl.ds(lo * GROUP * BLOCK, (end - lo * GROUP) * BLOCK))
        copies.append(pltpu.make_async_copy(hbm.at[where], buf.at[where], sems.at[c]))
        for copy in copies:
            copy.start()
        out.append(((lo, hi), *copies))
    return out


def picked(band, sel_ref, src_ref, dst_ref, top_ref, start, count):
    rows, tokens = sel_ref.shape
    runs = [(slice(0, rows), slice(0, tokens))]
    if band:
        runs = [
            (slice(r, min(r + LANES, rows)), slice(r, min(r + 2 * LANES, tokens)))
            for r in range(0, rows, LANES)
        ]
    tops = []
    for i in range(0, count, 2):
        width = min(2, count - i) * BLOCK
        at = pl.ds(start + i * BLOCK, width)
        got = jnp.concatenate(
            [
                jnp.dot(sel_ref[r, t], src_ref[t, at], preferred_element_type=F32)
                for r, t in runs
            ],
            axis=0,
        )
        dst_ref[:, at] = got.astype(BF16)
        tops += [got[:, j : j + BLOCK] for j in range(0, width, BLOCK)]
    top_ref[...] = functools.reduce(jnp.maximum, tops, top_ref[...])


def size_kernel(sizes, mask_ref, which_ref):
    kept = jnp.sum(mask_ref[...].reshape(1, -1).astype(F32))
    which = sum((kept > size).astype(jnp.int32) for size in sizes[:-1]) + 0
    if len(sizes) > 1:
        which = jnp.where(kept < mask_ref.shape[0] - LANES, len(sizes) - 1, which)
    which_ref[0] = which


def send_kernel(
    rows, first, band, sb_dev,
    me_ref, mask_ref, dest_hbm, x_hbm, w_hbm, s_hbm, send_ref, kept,
    x_buf, w_buf, s_buf, dest, sel, xc, maps, cols,
    top, total, s_top, s_total, used,
    in_sem, w_sem, x_sem, s_sem,
):
    blocks = w_buf.shape[0]
    s_blocks = s_buf.shape[1] // BLOCK
    peers = send_ref.shape[0]
    x_copies = column_copies(x_hbm, x_buf, x_sem, blocks, 3, (w_hbm, w_buf, w_sem))
    ((_, s_copy),) = column_copies(s_hbm, s_buf, s_sem, s_blocks, 1)
    dest_copy = pltpu.make_async_copy(dest_hbm, dest, in_sem)
    dest_copy.start()
    sel[...] = selector(mask_ref[...].reshape(1, -1), rows, first)
    top[...] = jnp.full(top.shape, -jnp.inf, F32)
    s_top[...] = jnp.full(top.shape, -jnp.inf, F32)
    total[...] = jnp.zeros(total.shape, F32)
    s_total[...] = jnp.zeros(total.shape, F32)

    def clear(i, carry):
        used[i] = 0
        return carry

    lax.fori_loop(0, peers, clear, 0)
    ones = jnp.ones((K * BLOCK, BLOCK), BF16)

    def weight(b):
        both = jnp.concatenate([w_buf[b, k] for k in range(K)], axis=1)
        scale = 1.0 / jnp.dot(both, ones, preferred_element_type=F32)
        maps[b] = (both.astype(F32) * jnp.concatenate([scale] * K, axis=1)).astype(BF16)

    def teacher(i, count):
        start = i * GROUP * BLOCK
        if not isinstance(i, int):
            start = pl.multiple_of(start, GROUP * BLOCK)
        picked(band, sel, x_buf, xc, top, start, count)
        for j in range(count):
            weight(i * GROUP + j)

    def teachers(i, carry):
        teacher(i, GROUP)
        return carry

    for (lo, hi), *copies in x_copies:
        for copy in copies:
            copy.wait()
        lax.fori_loop(lo, hi, teachers, 0)
    if blocks % GROUP:
        teacher(blocks // GROUP, blocks % GROUP)
    highest = jnp.max(top[...], axis=1, keepdims=True)
    top[...] = jnp.broadcast_to(highest, top.shape)
    dest_copy.wait()
    s_copy.wait()
    base = me_ref[0] * blocks
    factor = (1 << 16) // sb_dev + 1
    assert all(d * factor >> 16 == d // sb_dev for d in range(peers * sb_dev))
    lane = iota((8, LANES), 1)

    def raised(b):
        at = pl.ds(pl.multiple_of(b * BLOCK, BLOCK), BLOCK)
        return jnp.exp(xc[:, at].astype(F32) - top[...])

    def tile(b, value, route):
        mapped = jnp.dot(value.astype(BF16), maps[b], preferred_element_type=F32)
        for k in range(K):
            block = dest[k, base + b]
            owner = lax.shift_right_logical(block * factor, 16)
            rank = used[owner]
            used[owner] = rank + 1
            near = (block - owner * sb_dev).astype(F32)
            route = jnp.where(lane == owner * CAP + rank, near, route)
            at = pl.ds(pl.multiple_of(rank * rows, 16), rows)
            send_ref[owner, at] = mapped[:, k * BLOCK : (k + 1) * BLOCK].astype(BF16)
        return route

    def pair(i, route):
        one, two = raised(2 * i), raised(2 * i + 1)
        total[...] += one + two
        return tile(2 * i + 1, two, tile(2 * i, one, route))

    def both(i, route):
        picked(band, sel, s_buf, kept, s_top, pl.multiple_of(i * 4 * BLOCK, 4 * BLOCK), 4)
        return pair(2 * i + 1, pair(2 * i, route))

    shared = min(blocks, s_blocks) // 4 * 2
    route = lax.fori_loop(0, shared // 2, both, jnp.full((8, LANES), sb_dev, F32))
    for i in range(shared, blocks // 2):
        route = pair(i, route)
    for b in range(2 * shared, s_blocks, 2):
        picked(band, sel, s_buf, kept, s_top, b * BLOCK, min(2, s_blocks - b))
    if blocks % 2:
        last = raised(blocks - 1)
        total[...] += last
        route = tile(blocks - 1, last, route)
    summed = jnp.sum(total[...], axis=1, keepdims=True)
    s_highest = jnp.max(s_top[...], axis=1, keepdims=True)
    s_top[...] = jnp.broadcast_to(s_highest, top.shape)

    def student(start, count):
        at = [pl.ds(start + i * BLOCK, BLOCK) for i in range(count)]
        s_total[...] += sum(jnp.exp(kept[:, a].astype(F32) - s_top[...]) for a in at)

    def students(i, carry):
        student(pl.multiple_of(i * GROUP * BLOCK, GROUP * BLOCK), GROUP)
        return carry

    lax.fori_loop(0, s_blocks // GROUP, students, 0)
    if s_blocks % GROUP:
        student(s_blocks // GROUP * GROUP * BLOCK, s_blocks % GROUP)
    s_summed = jnp.sum(s_total[...], axis=1, keepdims=True)
    columns = (highest, *parted(summed, 2), s_highest, *parted(s_summed, 2))
    full, rest = divmod(rows, LANES)
    half = 0 < rest <= LANES // 2
    facts = fact_rows(rows)
    cols[...] = jnp.zeros(cols.shape, F32)
    cols[0:rows] = in_lanes(columns, rows)
    if half:
        upper = [column[full * LANES :] for column in columns[VALUES // 2 :]]
        cols[full * LANES + LANES // 2 : full * LANES + LANES // 2 + rest] = in_lanes(upper, rest)
    total[0:facts] = jnp.zeros((facts, LANES), F32)
    for q in range(full + (rest > 0)):
        turned = cols[q * LANES : (q + 1) * LANES].T
        height = VALUES // 2 if half and q == full else VALUES
        total[q * VALUES : q * VALUES + height] = turned[:height]
    total[facts - 1 : facts] = route[0:1]
    packed = total[0:facts].astype(BF16)
    for d in range(peers):
        send_ref[d, CAP * rows : CAP * rows + facts] = packed


def combine_kernel(
    rows, first,
    me_ref, mask_ref, recv_ref, s_ref, out_ref,
    facts32, share, near_vm, near, acc, cols, near_sem,
):
    peers = recv_ref.shape[0]
    blocks = s_ref.shape[1] // BLOCK
    spans = -(-rows // LANES)
    facts = fact_rows(rows)
    arrived = recv_ref[:, CAP * rows : CAP * rows + facts]
    facts32[...] = arrived.astype(F32).reshape(facts32.shape)

    def fact(row):
        return facts32[pl.ds(row, peers, stride=facts), :]

    lane = iota((peers, LANES), 1)
    routes = fact(facts - 1)
    slots = jnp.zeros((peers, LANES), F32)
    for r in range(CAP):
        mine = jnp.where(lane == me_ref[0] * CAP + r, routes, 0.0)
        slots = jnp.where(lane == r, jnp.sum(mine, axis=1, keepdims=True), slots)
    near_vm[...] = slots.astype(jnp.int32)
    near_copy = pltpu.make_async_copy(near_vm, near, near_sem)
    near_copy.start()
    for q in range(spans):
        if rows - q * LANES > LANES // 2:
            values = [fact(q * VALUES + v) for v in range(VALUES)]
        else:
            values = [fact(q * VALUES + v) for v in range(VALUES // 2)]
            values += [pltpu.roll(value, LANES // 2, 1) for value in values]
        highest, high, low, s_highest, s_high, s_low = values
        raised = jnp.exp(highest - jnp.max(highest, axis=0, keepdims=True))
        total = jnp.sum(raised * (high + low), axis=0, keepdims=True)
        part = raised * ((1.0 - SMOOTH) / total)
        s_top = jnp.max(s_highest, axis=0, keepdims=True)
        s_total = jnp.sum(jnp.exp(s_highest - s_top) * (s_high + s_low), axis=0, keepdims=True)
        norm = jnp.broadcast_to(s_top + jnp.log(s_total), (LANES - peers, LANES))
        share[q * LANES : (q + 1) * LANES] = jnp.concatenate([part, norm], axis=0).T
    cols[...] = jnp.zeros(cols.shape, F32)
    near_copy.wait()

    def work(start, chunk):
        at = pl.ds(start, chunk)
        inner = pl.ds(0, chunk)
        shares = share[at]
        acc[:, inner] = jnp.zeros((blocks + 1, chunk, LANES), F32)

        def sources(i, turned):
            for j in range(SOURCES):
                source = i * SOURCES + j
                scale = jnp.broadcast_to(turned[:, j : j + 1], (chunk, LANES))
                for r in range(CAP):
                    piece = recv_ref[source, pl.ds(r * rows + start, chunk)]
                    acc[near[source, r], inner] += scale * piece.astype(F32)
            return pltpu.roll(turned, LANES - SOURCES, 1)

        lax.fori_loop(0, peers // SOURCES, sources, shares)
        norm = jnp.broadcast_to(shares[:, peers : peers + 1], (chunk, LANES))

        def block(j, cross):
            target = acc[j, inner] + SMOOTH / VS
            start_of = j * BLOCK if isinstance(j, int) else pl.multiple_of(j * BLOCK, BLOCK)
            student = s_ref[at, pl.ds(start_of, BLOCK)].astype(F32)
            return cross + target * (jnp.log(target) - (student - norm))

        def step(i, cross):
            for j in range(STEP):
                cross = block(i * STEP + j, cross)
            return cross

        cross = lax.fori_loop(0, blocks // STEP, step, jnp.zeros((chunk, LANES), F32))
        for j in range(blocks // STEP * STEP, blocks):
            cross = block(j, cross)
        cols[at] = jnp.broadcast_to(jnp.sum(cross, axis=1, keepdims=True), (chunk, LANES))

    for start in range(0, rows, acc.shape[1]):
        work(start, min(acc.shape[1], rows - start))
    counted = jnp.sum(mask_ref[...].reshape(1, -1).astype(F32), axis=1, keepdims=True)
    row = iota((8, LANES), 0)
    place = iota((8, LANES), 1)
    values = jnp.zeros((8, LANES), F32)
    part = jnp.zeros((8, LANES), F32)
    for q in range(spans):
        kl = cols[q * LANES : (q + 1) * LANES].T[:8]
        ahead = place + q * LANES
        kl = jnp.where((ahead < rows) & ((ahead + first).astype(F32) < counted), kl, 0.0)
        values = jnp.where(row % 4 == q, kl, values)
        part = part + kl
    whole_sum = jnp.broadcast_to(jnp.sum(part, axis=1, keepdims=True), (8, LANES))
    tally = jnp.where(place == 0, whole_sum, jnp.where(place == 1, counted, 0.0))
    values = jnp.where(row % 4 == 3, tally, values)
    for d in range(peers // 2):
        out_ref[d * 8 : (d + 1) * 8] = values


def tally_kernel(all_ref, out_ref):
    peers = all_ref.shape[0] // 4
    sums = jnp.sum(all_ref[pl.ds(3, peers, stride=4), :], axis=0, keepdims=True)
    lane = iota((1, LANES), 1)
    sums = jnp.where(lane == 1, sums * (1.0 / peers), sums)
    out_ref[...] = jnp.broadcast_to(sums, out_ref.shape)


def loss_kernel(rows, first, all_ref, mask_ref, loss_ref):
    peers = all_ref.shape[0] // 4
    spans = -(-rows // LANES)
    kl = jnp.concatenate(
        [
            jnp.sum(all_ref[pl.ds(q, peers, stride=4), :], axis=0, keepdims=True)
            for q in range(spans)
        ],
        axis=1,
    )
    mask = mask_ref[...].reshape(1, -1)
    width = spans * LANES
    row = iota((16, width), 0)
    parts = jnp.zeros((16, width), F32)
    for v, part in enumerate(parted(kl, 3)):
        parts = jnp.where(row == v, jnp.broadcast_to(part, (16, width)), parts)
    back = jnp.dot(parts.astype(BF16), selector(mask, width, first), preferred_element_type=F32)
    loss = jnp.sum(back, axis=0, keepdims=True) * mask.astype(F32)
    loss_ref[...] = loss.reshape(loss_ref.shape)


def close_kernel(tally_ref, mean_ref):
    lane = iota((1, LANES), 1)
    sums = jnp.sum(tally_ref[...], axis=0, keepdims=True)
    total = jnp.sum(jnp.where(lane == 0, sums, 0.0), axis=1, keepdims=True)
    count = jnp.sum(jnp.where(lane == 1, sums, 0.0), axis=1, keepdims=True)
    mean_ref[0] = jnp.sum(total / count)


def whole(memory_space):
    return pl.BlockSpec(memory_space=memory_space)


VM, SM, HB = pltpu.VMEM, pltpu.SMEM, pltpu.HBM
SMALL = pltpu.CompilerParams(vmem_limit_bytes=6 << 20)


def exchanged(rows, band, teacher_logits, student_logits, dest, tile_weight, mask):
    first = 0
    peers = lax.axis_size("vocab")
    groups = lax.axis_size("dp")
    me = lax.axis_index("vocab").astype(jnp.int32).reshape(1)
    tokens = teacher_logits.shape[0]
    tb_dev = teacher_logits.shape[1] // BLOCK
    sb_dev = student_logits.shape[1] // BLOCK
    wide = -(-rows // LANES) * LANES
    facts = fact_rows(rows)
    dma = pltpu.SemaphoreType.DMA
    tall = max(rows, LANES)
    send, kept = pl.pallas_call(
        functools.partial(send_kernel, rows, first, band, sb_dev),
        out_shape=(
            jax.ShapeDtypeStruct((peers, CAP * rows + facts, LANES), BF16),
            jax.ShapeDtypeStruct((rows, student_logits.shape[1]), BF16),
        ),
        in_specs=[whole(SM), whole(VM), whole(HB), whole(HB), whole(HB), whole(HB)],
        out_specs=(whole(VM), whole(VM)),
        scratch_shapes=[
            VM(teacher_logits.shape, BF16),
            VM(tile_weight.shape, BF16),
            VM(student_logits.shape, BF16),
            SM(dest.shape, jnp.int32),
            VM((rows, tokens), BF16),
            VM((rows, tb_dev * BLOCK), BF16),
            VM((tb_dev, BLOCK, K * BLOCK), BF16),
            VM((wide, LANES), F32),
            VM((rows, LANES), F32),
            VM((rows, LANES), F32),
            VM((rows, LANES), F32),
            VM((rows, LANES), F32),
            SM((peers,), jnp.int32),
            dma(()),
            dma((3,)),
            dma((3,)),
            dma((1,)),
        ],
        compiler_params=pltpu.CompilerParams(vmem_limit_bytes=34 << 20),
        name="send",
    )(me, mask, dest, teacher_logits, tile_weight, student_logits)
    received = lax.all_to_all(send, "vocab", 0, 0, tiled=True)
    chunk = -(-rows // 32) * 16
    mine = pl.pallas_call(
        functools.partial(combine_kernel, rows, first),
        out_shape=jax.ShapeDtypeStruct((peers * 4, LANES), F32),
        in_specs=[whole(SM), whole(VM), whole(VM), whole(VM)],
        out_specs=whole(VM),
        scratch_shapes=[
            VM((peers * facts, LANES), F32),
            VM((wide, LANES), F32),
            VM((peers, LANES), jnp.int32),
            SM((peers, LANES), jnp.int32),
            VM((sb_dev + 1, chunk, LANES), F32),
            VM((wide, LANES), F32),
            dma(()),
        ],
        compiler_params=pltpu.CompilerParams(vmem_limit_bytes=20 << 20),
        name="combine",
    )(me, mask, received, kept)
    collected = lax.all_to_all(mine, "vocab", 0, 0, tiled=True)
    tally = pl.pallas_call(
        tally_kernel,
        out_shape=jax.ShapeDtypeStruct((groups, LANES), F32),
        in_specs=[whole(VM)],
        out_specs=whole(VM),
        compiler_params=SMALL,
        name="tally",
    )(collected)
    loss = pl.pallas_call(
        functools.partial(loss_kernel, rows, first),
        out_shape=jax.ShapeDtypeStruct((tokens,), F32),
        in_specs=[whole(VM), whole(VM)],
        out_specs=whole(VM),
        cost_estimate=pl.CostEstimate(flops=10**10, bytes_accessed=10**6, transcendentals=0),
        compiler_params=SMALL,
        name="loss",
    )(collected, mask)
    return loss, tally


def local(teacher_logits, student_logits, tile_dest, tile_weight, token_mask):
    tokens = teacher_logits.shape[0]
    parts = (teacher_logits, student_logits, tile_dest.T, tile_weight, token_mask)
    sizes = [tokens]
    if tokens % 384 == 0:
        sizes = [tokens // 384 * size for size in (304, 320, 384)]
    which = pl.pallas_call(
        functools.partial(size_kernel, sizes),
        out_shape=jax.ShapeDtypeStruct((1,), jnp.int32),
        in_specs=[whole(VM)],
        out_specs=whole(SM),
        compiler_params=SMALL,
        name="size",
    )(token_mask)
    loss, tally = lax.switch(which.reshape(()), [functools.partial(exchanged, size, size < tokens) for size in sizes], *parts)
    tally = lax.all_to_all(tally, "dp", 0, 0, tiled=True)
    mean = pl.pallas_call(
        close_kernel,
        out_shape=jax.ShapeDtypeStruct((1,), F32),
        in_specs=[whole(VM)],
        out_specs=whole(SM),
        compiler_params=SMALL,
        name="close",
    )(tally)
    return loss, mean.reshape(())


def solution(mesh):
    in_specs = (P("dp", "vocab"), P("dp", "vocab"), P(), P("vocab", None, None, None), P("dp"))
    out_specs = (P("dp"), P())
    return jax.shard_map(local, mesh=mesh, in_specs=in_specs, out_specs=out_specs, check_vma=False)
```
